128 devices in a mesh: stripe: 32 (over x, y_lo, z), sub: 4 (over y_hi, core).
Axes of the slice: x: 4, y: 4 (y_hi: 2, y_lo: 2; y = y_hi * 2 + y_lo), z: 4, core: 2. Of those that a mesh axis runs over, the one named last changes fastest.
Arguments:
- channel: float32 [8, 32, 64, 512], P('sub', 'stripe'), may hold values from -0.25 to 0.25
- received: float32 [8, 32, 2048], P('sub', None, 'stripe'), may hold values from -18 to 18
- noise_var: float32 [8, 32], P('sub', 'stripe'), may hold values from 0.25 to 4
- downlink: float32 [8, 32, 512], P('sub'), may hold values from -6 to 6
- user_order: int32 [512], P('stripe'), may hold values from 0 to 511, each once
Outputs:
- transmit: float32 [8, 32, 2048], P('sub', None, 'stripe')
- owned: float32 [8, 32, 512], P('sub', None, 'stripe')
The draws below stay inside these ranges and needn't reach their ends.
Inputs may be any that keep to these rules, and one draw needn't show every extreme that they name: `user_order`: a permutation of the 512 users.
All inputs are finite; a program needn't handle non-finite values.
Results may differ from the reference program's by a relative error of at most 0.00017.
Values sent between devices are 32-bit elements; how exact they have to be, the bound alone decides.
No kernel may reach another device: no remote copies, remote signals or barrier semaphores. Data moves between devices by JAX's collectives and lax.ppermute only.
A program may use at most 256 MiB of HBM per device.

```python
import math
import jax
import jax.numpy as jnp
from jax import lax

K = 512
M = 64
S = 32
NB = 8
L = 32


def level_of(own_key, shape, cuts, least, top_value):
    def one(dim, blocks):
        heights = jax.random.uniform(jax.random.fold_in(jax.random.fold_in(own_key, 6), dim), (blocks,), jnp.float32, least / len(cuts), top_value / len(cuts))
        return jnp.repeat(jnp.exp(heights), shape[dim] // blocks).reshape((-1,) + (1,) * (len(shape) - dim - 1))

    factor_of = one(*cuts[0])
    for cut in cuts[1:]:
        factor_of = factor_of * one(*cut)
    return factor_of


def noise(key, dims, deviation, most, pieces=(), kind=jnp.bfloat16):
    entries = deviation * jax.random.normal(key, dims, jnp.float32)
    if pieces:
        entries = entries * level_of(key, dims, pieces, -0.22, 0.18)
    return jnp.clip(entries, -most, most).astype(kind)


def setup_inputs(seed: int = 0) -> dict:
    key_of = jax.random.split(jax.random.key(seed), 6)
    return {
        "channel": noise(key_of[0], (NB, L, M, K), K ** -0.5, 0.25, ((0, 4), (1, 32)), jnp.float32),
        "received": noise(key_of[1], (NB, S, L * M), 3.0, 18.0, ((0, 4), (2, 32)), jnp.float32),
        "noise_var": jnp.clip(jnp.exp(math.log(4.0) - 2.7725887 * jax.random.uniform(key_of[2], (NB, L), jnp.float32) ** level_of(key_of[2], (NB, L), ((0, 4), (1, 32)), -0.2, 0.2)), 0.25, 4.0),
        "downlink": noise(key_of[3], (NB, S, K), 1.0, 6.0, ((0, 4),), jnp.float32),
        "user_order": jax.random.permutation(key_of[4], K).astype(jnp.int32),
    }


prior_var = 0.1

def product(left, right):
    return jnp.dot(left.astype(jnp.float32), right.astype(jnp.float32), precision=lax.Precision.HIGHEST, preferred_element_type=jnp.float32)

def woodbury(covariance, estimate, matrix, samples, variance):
    cross_term = product(covariance, matrix.T)
    system = product(matrix, cross_term) + variance * jnp.eye(matrix.shape[0], dtype=jnp.float32)
    factor = jnp.linalg.cholesky(system)
    gain_rows = jax.scipy.linalg.cho_solve((factor, True), cross_term.T)
    residual_rows = samples - product(estimate, matrix.T)
    estimate = estimate + product(residual_rows, gain_rows)
    covariance = covariance - product(cross_term, gain_rows)
    return (covariance, estimate)

def reference(channel, received, noise_var, downlink, user_order):
    blocks, link_count, antennas, user_count = channel.shape
    symbols = received.shape[1]
    samples = received.reshape(blocks, symbols, link_count, antennas).transpose(0, 2, 1, 3)

    def one_block(inputs):

        def advance(carried, per_link):
            return (woodbury(carried[0], carried[1], per_link[0], per_link[1], per_link[2]), None)
        initial = (prior_var * jnp.eye(user_count, dtype=jnp.float32), jnp.zeros((symbols, user_count), jnp.float32))
        final_state, unused = lax.scan(advance, initial, inputs)
        return final_state
    covars, estimates = lax.map(one_block, (channel, samples, noise_var))
    mean_error = lax.optimization_barrier(jnp.mean(jnp.diagonal(covars, axis1=1, axis2=2), axis=0))
    power_scale = lax.rsqrt(mean_error)
    precoded = jnp.einsum('bsk,bkn->bsn', downlink, covars, precision=lax.Precision.HIGHEST) * power_scale
    transmit = jnp.einsum('bsk,blmk->bslm', precoded, channel, precision=lax.Precision.HIGHEST)
    transmit = transmit.reshape(blocks, symbols, link_count * antennas)
    owned_rows = jnp.take(estimates, user_order, axis=2)
    return (transmit, owned_rows)
```

```python
import functools

import jax
import jax.numpy as jnp
from jax import lax
from jax.experimental import pallas as pl
from jax.experimental.pallas import tpu as pltpu
from jax.sharding import PartitionSpec as P

prior_var = 0.1
TILE = 128
F32, BF16 = jnp.float32, jnp.bfloat16


def mm(left, right, dims=((1,), (0,))):
    return lax.dot_general(left, right, (dims, ((), ())), preferred_element_type=F32)


def exact(left, right):
    return jnp.dot(left, right, precision=lax.Precision.HIGHEST, preferred_element_type=F32)


def split(value):
    high = value.astype(BF16)
    return high, (value - high.astype(F32)).astype(BF16)


def prepare(pick_ref, channel_ref, received_ref, noise_ref, keep_ref, give_ref):
    mine = pick_ref[0]
    users = channel_ref.shape[-1]
    for which, out_ref in ((mine, keep_ref), (1 - mine, give_ref)):
        scale = 1.0 / jnp.sqrt(jnp.full((1, 1), noise_ref[which, 0], F32))
        out_ref[:, :users] = channel_ref[which] * scale
        out_ref[:, users:] = jnp.zeros(out_ref[:, users:].shape, F32)
        samples = received_ref[which].T
        out_ref[:, users : users + samples.shape[1]] = samples * scale


def gram(keep_ref, take_ref, out_ref):
    users, symbols = keep_ref.shape[1] - TILE, 32
    both = jnp.concatenate([keep_ref[...], take_ref[...]], axis=0)
    high, low = split(both)
    left = jnp.concatenate([high, high, low], axis=0).T
    right = jnp.concatenate([high, low, high], axis=0)
    tiles, at = users // TILE, 0
    for i in range(tiles):
        row = mm(left[i * TILE : (i + 1) * TILE], right[:, : (i + 1) * TILE])
        for j in range(i + 1):
            out_ref[at : at + TILE] = row[:, j * TILE : (j + 1) * TILE]
            at += TILE
    row = mm(left[users : users + symbols], right[:, :users])
    for j in range(tiles):
        out_ref[at : at + symbols] = row[:, j * TILE : (j + 1) * TILE]
        at += symbols


def eye_of(n):
    return lax.broadcasted_iota(jnp.int32, (n, n), 0) == lax.broadcasted_iota(jnp.int32, (n, n), 1)


def step_count(error):
    def more(state):
        return (state[1] > 0.0125) & (state[0] < 40)

    def step(state):
        square = state[1] * state[1]
        return state[0] + 1, square / (2.0 - square)

    return lax.while_loop(more, step, (jnp.int32(0), error))[0]


def invert(gram_ref, downlink_ref, rows_ref, diag_ref, a_ref, x_ref, e_ref, v_ref):
    n, symbols = a_ref.shape[0], downlink_ref.shape[0]
    tiles, at = n // TILE, 0
    prior = 1.0 / prior_var
    for i in range(tiles):
        for j in range(i + 1):
            tile = gram_ref[at : at + TILE]
            at += TILE
            if i == j:
                tile = tile + jnp.where(eye_of(TILE), prior, 0.0)
            else:
                a_ref[j * TILE : (j + 1) * TILE, i * TILE : (i + 1) * TILE] = tile.T
            a_ref[i * TILE : (i + 1) * TILE, j * TILE : (j + 1) * TILE] = tile
    mixed = jnp.concatenate([gram_ref[at + symbols * j : at + symbols * (j + 1)] for j in range(tiles)], axis=1)
    rows = jnp.concatenate([downlink_ref[...], mixed], axis=0)
    a = a_ref[...]
    eye = jnp.where(eye_of(n), 1.0, 0.0)
    top = jnp.max(jnp.sum(jnp.abs(a), axis=1)) * 1.0001
    alpha = 2.0 / (prior + top)
    start = (top - prior) / (top + prior)
    square = start * start
    gain, bound = 2.0 / (2.0 - square), square / (2.0 - square)
    first = (2.0 * alpha * gain) * eye - (alpha * alpha * gain) * a
    count = step_count(bound)
    a_high, a_low = split(a)
    x_ref[...] = first.astype(BF16)

    def step(index, bound):
        x = x_ref[...]
        left = (eye - mm(a_high, x)).astype(BF16)
        square = bound * bound
        gain = 2.0 / (2.0 - square)
        x_ref[...] = ((x.astype(F32) + mm(x, left)) * gain).astype(BF16)
        return square / (2.0 - square)

    lax.fori_loop(0, jnp.minimum(count, 6), step, bound)
    x = x_ref[...]
    error = eye - (mm(a_high, x) + mm(a_low, x))
    e = error.astype(BF16)
    twice = mm(e, e)
    e_ref[...] = error
    v_ref[...] = twice
    good = jnp.sum(twice * twice) < 1e-5

    @pl.when(good)
    def _():
        error = e_ref[...]
        twice = v_ref[...]
        e = error.astype(BF16)
        x = x_ref[...]
        update = mm(x, e)
        diag = jnp.where(eye_of(n), x.astype(F32) + update, 0.0) + (error + twice) * update
        diag_ref[...] = jnp.broadcast_to(jnp.sum(diag, axis=0)[None, None], diag_ref.shape)
        high, low = split(rows)
        z = mm(jnp.concatenate([high, low], axis=0), x)
        z = z[: 2 * symbols] + z[2 * symbols :]
        z = z + mm(z.astype(BF16), e)
        rows_ref[...] = z + mm(z.astype(BF16), twice.astype(BF16))

    @pl.when(jnp.logical_not(good))
    def _():
        e_ref[...] = first

        def step(index, bound):
            x = e_ref[...]
            square = bound * bound
            gain = 2.0 / (2.0 - square)
            e_ref[...] = (x + exact(x, eye - exact(a_ref[...], x))) * gain
            return square / (2.0 - square)

        lax.fori_loop(0, count + 2, step, bound)
        x = e_ref[...]
        diag = jnp.sum(jnp.where(eye_of(n), x, 0.0), axis=0)
        diag_ref[...] = jnp.broadcast_to(diag[None, None], diag_ref.shape)
        rows_ref[...] = exact(rows, x)


def finish(pick_ref, own_ref, other_ref, diag_ref, channel_ref, order_ref, transmit_ref, owned_ref):
    mine = pick_ref[0]
    blocks, symbols = transmit_ref.shape[0], transmit_ref.shape[1]
    mean_error = jnp.sum(diag_ref[...], axis=0) / diag_ref.shape[0]
    scale = lax.rsqrt(mean_error)
    scale = scale * (1.5 - 0.5 * mean_error * scale * scale)
    n = own_ref.shape[1]
    order = order_ref[...]
    pick = (lax.broadcasted_iota(jnp.int32, (n, order.shape[1]), 0) == order).astype(BF16)
    for block in range(blocks):
        z = jnp.where(mine == block, own_ref[...], other_ref[...])
        high, low = split(z[:symbols] * scale)
        h_high, h_low = split(channel_ref[block])
        left = jnp.concatenate([high, low], axis=0)
        one = mm(left, h_high, ((1,), (1,)))
        two = mm(high, h_low, ((1,), (1,)))
        transmit_ref[block] = one[:symbols] + (one[symbols:] + two)
        x = z[symbols:]
        high = x.astype(BF16)
        rest = x - high.astype(F32)
        middle, low = split(rest)
        parts = mm(jnp.concatenate([high, middle, low], axis=0), pick)
        owned_ref[block] = parts[:symbols] + (parts[symbols : 2 * symbols] + parts[2 * symbols :])


VMEM = pl.BlockSpec(memory_space=pltpu.VMEM)
SMEM = pl.BlockSpec(memory_space=pltpu.SMEM)


def call(body, outs, in_specs, name, scratch=()):
    return pl.pallas_call(
        body,
        out_shape=outs,
        in_specs=in_specs,
        out_specs=jax.tree.map(lambda _: VMEM, outs),
        scratch_shapes=scratch,
        name=name,
        compiler_params=pltpu.CompilerParams(vmem_limit_bytes=48 << 20),
    )


def shards(channel, received, noise_var, downlink, user_order):
    blocks, _, antennas, n = channel.shape
    symbols = received.shape[1]
    channel = channel.reshape(blocks, antennas, n)
    links, subs = lax.axis_size("stripe"), lax.axis_size("sub")
    pair, ring = 4, links // 8
    position = lax.axis_index("stripe")
    mine = (position // pair) % 2
    pick = mine.reshape(1).astype(jnp.int32)
    planes = [[x * 8 + y * pair + z for x in range(ring) for z in range(pair)] for y in range(2)]
    columns = [
        [(x * 8 + y * pair + z) * subs + s for y in range(2) for s in range(subs)]
        for x in range(ring)
        for z in range(pair)
    ]
    swap = [(i, i ^ pair) for i in range(links)]

    def struct(*shape):
        return jax.ShapeDtypeStruct(shape, F32)

    keep, give = call(prepare, (struct(antennas, n + TILE),) * 2, [SMEM, VMEM, VMEM, SMEM], "prepare")(
        pick, channel, received, noise_var
    )
    take = lax.ppermute(give, "stripe", swap)
    tiles = n // TILE
    height = tiles * (tiles + 1) // 2 * TILE + tiles * symbols
    group = len(planes[0])
    part = call(gram, struct(height, TILE), [VMEM, VMEM], "gram")(keep, take)
    part = part.reshape(group, height // group, TILE)
    part = lax.all_to_all(part, "stripe", 0, 0, axis_index_groups=planes, tiled=True)
    part = jnp.broadcast_to(jnp.sum(part, axis=0), part.shape)
    whole = lax.all_to_all(part, "stripe", 0, 0, axis_index_groups=planes, tiled=True)
    whole = whole.reshape(height, TILE)
    down = lax.dynamic_index_in_dim(downlink, mine, 0, keepdims=False)
    column = len(columns[0])
    rows, diag = call(
        invert,
        (struct(2 * symbols, n), struct(column, 1, n)),
        [VMEM, VMEM],
        "invert",
        [pltpu.VMEM((n, n), F32), pltpu.VMEM((n, n), BF16), pltpu.VMEM((n, n), F32), pltpu.VMEM((n, n), F32)],
    )(whole, down)
    other = lax.ppermute(rows, "stripe", swap)
    diags = lax.all_to_all(diag, ("stripe", "sub"), 0, 0, axis_index_groups=columns, tiled=True)
    return call(
        finish,
        (struct(blocks, symbols, antennas), struct(blocks, symbols, user_order.shape[0])),
        [SMEM, VMEM, VMEM, VMEM, VMEM, VMEM],
        "finish",
    )(pick, rows, other, diags, channel, user_order.reshape(1, -1))


def solution(mesh):
    return jax.shard_map(
        shards,
        mesh=mesh,
        in_specs=(
            P("sub", "stripe", None, None),
            P("sub", None, "stripe"),
            P("sub", "stripe"),
            P("sub", None, None),
            P("stripe"),
        ),
        out_specs=(P("sub", None, "stripe"), P("sub", None, "stripe")),
        check_vma=False,
    )
```

```python
import functools

import jax
import jax.numpy as jnp
from jax import lax
from jax.experimental import pallas as pl
from jax.experimental.pallas import tpu as pltpu
from jax.sharding import PartitionSpec as P


prior_var = 0.1
TILE = 128
F32, BF16 = jnp.float32, jnp.bfloat16


def mm(left, right, dims=((1,), (0,))):
    return lax.dot_general(left, right, (dims, ((), ())), preferred_element_type=F32)


def exact(left, right):
    return jnp.dot(left, right, precision=lax.Precision.HIGHEST, preferred_element_type=F32)


def split(value):
    high = value.astype(BF16)
    return high, (value - high.astype(F32)).astype(BF16)


def enter(pick_ref, channel_ref, received_ref, noise_ref, order_ref, keep_ref, give_ref, kept_ref, samples, noise, sems):
    mine = pick_ref[0]
    antennas = channel_ref.shape[1]
    sides = ((mine, keep_ref), (1 - mine, give_ref))
    copies = [
        pltpu.make_async_copy(received_ref, samples, sems.at[0]),
        pltpu.make_async_copy(noise_ref, noise, sems.at[1]),
        pltpu.make_async_copy(order_ref, kept_ref, sems.at[2]),
    ] + [
        pltpu.make_async_copy(channel_ref.at[which], out_ref.at[pl.ds(0, antennas)], sems.at[3 + k])
        for k, (which, out_ref) in enumerate(sides)
    ]
    for copy in copies:
        copy.start()
    for copy in copies[:2]:
        copy.wait()
    for which, out_ref in sides:
        out_ref[antennas:] = jnp.full((8, out_ref.shape[1]), noise[which], F32)
        for k in range(samples.shape[1] // 8):
            out_ref[antennas:, k * TILE : k * TILE + antennas] = samples[which, 8 * k : 8 * k + 8]
    for copy in copies[2:]:
        copy.wait()


def gram(symbols, keep_ref, take_ref, out_ref):
    antennas, users = keep_ref.shape[0] - 8, keep_ref.shape[1]

    def scaled(ref):
        extra = ref[antennas:]
        scale = 1.0 / jnp.sqrt(extra[:1, antennas : antennas + 1])
        chunks = [extra[:, k * TILE : k * TILE + antennas] for k in range(symbols // 8)]
        return ref[:antennas] * scale, jnp.concatenate(chunks, axis=0) * scale

    own, own_samples = scaled(keep_ref)
    other, other_samples = scaled(take_ref)
    both = jnp.concatenate([own, other], axis=0)
    samples = jnp.concatenate([own_samples, other_samples], axis=1)
    high, low = split(both)
    left = jnp.concatenate([high, high, low], axis=0).T
    right = jnp.concatenate([high, low, high], axis=0)
    y_high, y_low = split(samples)
    mixed = mm(jnp.concatenate([y_high, y_high, y_low], axis=1), right)
    tiles, at = users // TILE, 0
    lower = lower_of(TILE)
    diagonal = []
    for i in range(tiles):
        row = mm(left[i * TILE : (i + 1) * TILE], right[:, : (i + 1) * TILE])
        for j in range(i):
            out_ref[at : at + TILE] = row[:, j * TILE : (j + 1) * TILE]
            at += TILE
        diagonal.append(row[:, i * TILE :])
    for i in range(0, tiles, 2):
        out_ref[at : at + TILE] = jnp.where(lower, diagonal[i], diagonal[i + 1])
        at += TILE
    for j in range(tiles):
        out_ref[at : at + symbols] = mixed[:, j * TILE : (j + 1) * TILE]
        at += symbols
    out_ref[at:] = jnp.zeros((out_ref.shape[0] - at, TILE), F32)
    for i in range(1, tiles, 2):
        out_ref[at : at + 1] = jnp.sum(jnp.where(eye_of(TILE), diagonal[i], 0.0), axis=0, keepdims=True)
        at += 1


def lower_of(n):
    return lax.broadcasted_iota(jnp.int32, (n, n), 0) >= lax.broadcasted_iota(jnp.int32, (n, n), 1)


def eye_of(n):
    return lax.broadcasted_iota(jnp.int32, (n, n), 0) == lax.broadcasted_iota(jnp.int32, (n, n), 1)


def step_count(error):
    def more(state):
        return (state[1] > 0.0125) & (state[0] < 40)

    def step(state):
        return state[0] + 1, after(state[1])

    return lax.while_loop(more, step, (jnp.int32(0), error))[0]


def after(bound):
    square = bound * bound
    return square / (2.0 - square)


def gain_of(bound):
    return 2.0 / (2.0 - bound * bound)


def invert(symbols, gram_ref, diag_ref, flag_ref, x_ref, e_ref, v_ref, a_ref, s_ref, t_ref):
    n = a_ref.shape[0]
    tiles, at = n // TILE, 0
    prior = 1.0 / prior_var
    lower, middle = lower_of(TILE), eye_of(TILE)
    tail = tiles * tiles // 2 * TILE + tiles * symbols

    def put(i, j, tile):
        a_ref[i * TILE : (i + 1) * TILE, j * TILE : (j + 1) * TILE] = tile

    for i in range(tiles):
        for j in range(i):
            tile = gram_ref[at : at + TILE]
            at += TILE
            put(i, j, tile)
            put(j, i, tile.T)
    for i in range(0, tiles, 2):
        tile = gram_ref[at : at + TILE]
        at += TILE
        flip = tile.T
        put(i, i, jnp.where(lower, tile, flip) + jnp.where(middle, prior, 0.0))
        row = gram_ref[tail + i // 2 : tail + i // 2 + 1] + prior
        put(i + 1, i + 1, jnp.where(middle, row, jnp.where(lower, flip, tile)))
    a = a_ref[...]
    eye = jnp.where(eye_of(n), 1.0, 0.0)
    top = jnp.max(jnp.sum(jnp.abs(a), axis=1)) * 1.0001
    alpha = 2.0 / (prior + top)
    start = (top - prior) / (top + prior)
    count = step_count(after(start))
    left = (eye - alpha * a).astype(BF16)
    s_ref[n:] = ((alpha * gain_of(start)) * (eye + left.astype(F32))).astype(BF16)

    def squared(product, bound):
        square = bound * bound
        return ((2.0 * product - square * eye) / (2.0 - square)).astype(BF16)

    s_ref[:n] = squared(mm(left, left), start)

    def step(index, bound):
        both = mm(s_ref[...], s_ref[:n])
        s_ref[n:] = (gain_of(bound) * (s_ref[n:].astype(F32) + both[n:])).astype(BF16)
        s_ref[:n] = squared(both[:n], bound)
        return after(bound)

    bound = lax.fori_loop(0, jnp.minimum(count, 7) - 1, step, after(start))
    x = s_ref[n:]
    x = (gain_of(bound) * (x.astype(F32) + mm(x, s_ref[:n]))).astype(BF16)
    x_ref[...] = x
    a_high, a_low = split(a)
    parts = mm(jnp.concatenate([a_high, a_low], axis=0), x)
    error = eye - (parts[:n] + parts[n:])
    e = error.astype(BF16)
    e_ref[...] = e
    both = mm(jnp.concatenate([e, x], axis=0), e)
    twice, update = both[:n], both[n:]
    v_ref[...] = twice.astype(BF16)
    diag = jnp.where(eye_of(n), x.astype(F32) + update, 0.0) + (error + twice) * update
    diag_ref[...] = jnp.sum(diag, axis=0, keepdims=True)
    good = jnp.sum(twice * twice) < 3e-5
    flag_ref[0] = good.astype(jnp.int32)

    @pl.when(jnp.logical_not(good))
    def _():
        a = a_ref[...]
        t_ref[...] = (alpha * gain_of(start)) * (2.0 * eye - alpha * a)

        def step(index, bound):
            x = t_ref[...]
            t_ref[...] = (x + exact(x, eye - exact(a_ref[...], x))) * gain_of(bound)
            return after(bound)

        lax.fori_loop(0, count + 2, step, after(start))
        x = t_ref[...]
        diag_ref[...] = jnp.sum(jnp.where(eye_of(n), x, 0.0), axis=0, keepdims=True)
        x_ref[...] = x.astype(BF16)
        e_ref[...], v_ref[...] = split(x - x.astype(BF16).astype(F32))


def apply(pick_ref, flag_ref, gram_ref, downlink_ref, x_ref, e_ref, v_ref, rows_ref):
    symbols, n = downlink_ref.shape[1:]
    tiles = n // TILE
    at = tiles * tiles // 2 * TILE
    mixed = jnp.concatenate([gram_ref[at + symbols * j : at + symbols * (j + 1)] for j in range(tiles)], axis=1)
    rows = jnp.concatenate([downlink_ref[pick_ref[0]], mixed], axis=0)
    good = flag_ref[0] == 1

    @pl.when(good)
    def _():
        high, low = split(rows)
        z = mm(jnp.concatenate([high, low], axis=0), x_ref[...])
        z = z[: 2 * symbols] + z[2 * symbols :]
        z = z + mm(z.astype(BF16), e_ref[...])
        rows_ref[...] = z + mm(z.astype(BF16), v_ref[...])

    @pl.when(jnp.logical_not(good))
    def _():
        x = x_ref[...].astype(F32) + (e_ref[...].astype(F32) + v_ref[...].astype(F32))
        rows_ref[...] = exact(rows, x)


def finish(terms, pick_ref, own_ref, other_ref, diag_ref, channel_ref, order_ref, transmit_ref, owned_ref):
    mine = pick_ref[0]
    blocks, symbols = transmit_ref.shape[0], transmit_ref.shape[1]
    mean_error = diag_ref[...] / terms
    scale = lax.rsqrt(mean_error)
    scale = scale * (1.5 - 0.5 * mean_error * scale * scale)
    n = own_ref.shape[1]
    order = order_ref[...]
    pick = (lax.broadcasted_iota(jnp.int32, (n, order.shape[1]), 0) == order).astype(BF16)
    for block in range(blocks):
        z = jnp.where(mine == block, own_ref[...], other_ref[...])
        high, low = split(z[:symbols] * scale)
        h_high, h_low = split(channel_ref[block])
        left = jnp.concatenate([high, low], axis=0)
        one = mm(left, h_high, ((1,), (1,)))
        two = mm(high, h_low, ((1,), (1,)))
        transmit_ref[block] = one[:symbols] + (one[symbols:] + two)
        x = z[symbols:]
        high = x.astype(BF16)
        rest = x - high.astype(F32)
        middle, low = split(rest)
        parts = mm(jnp.concatenate([high, middle, low], axis=0), pick)
        owned_ref[block] = (parts[:symbols] + (parts[symbols : 2 * symbols] + parts[2 * symbols :])).T


VMEM = pl.BlockSpec(memory_space=pltpu.VMEM)
SMEM = pl.BlockSpec(memory_space=pltpu.SMEM)


HBM = pl.BlockSpec(memory_space=pltpu.HBM)


def call(body, outs, in_specs, scratch=(), grant=48 << 20, outs_in=None, flops=None):
    return pl.pallas_call(
        body,
        out_shape=outs,
        in_specs=in_specs,
        out_specs=outs_in or jax.tree.map(lambda _: VMEM, outs),
        cost_estimate=flops and pl.CostEstimate(flops=flops, bytes_accessed=2 << 20, transcendentals=0),
        scratch_shapes=scratch,
        compiler_params=pltpu.CompilerParams(vmem_limit_bytes=grant),
    )


def shards(channel, received, noise_var, downlink, user_order):
    blocks, _, antennas, n = channel.shape
    symbols = received.shape[1]
    channel = channel.reshape(blocks, antennas, n)
    noise_var = noise_var.reshape(blocks)
    order = user_order.reshape(1, -1)
    links, subs = lax.axis_size("stripe"), lax.axis_size("sub")
    pair, ring = 4, links // 8
    mine = (lax.axis_index("stripe") // pair) % 2
    pick = mine.reshape(1).astype(jnp.int32)
    planes = [[x * 8 + y * pair + z for x in range(ring) for z in range(pair)] for y in range(2)]
    swap = [(i, i ^ pair) for i in range(links)]
    cores = [(i, i ^ 1) for i in range(subs)]
    across = [(i * subs + s, (i ^ pair) * subs + (s ^ 2)) for i in range(links) for s in range(subs)]

    def struct(*shape):
        return jax.ShapeDtypeStruct(shape, F32)

    def outside(value):
        return pltpu.with_memory_space_constraint(value, pltpu.HBM)

    keep, give, order = call(
        enter,
        (struct(antennas + 8, n), struct(antennas + 8, n), jax.ShapeDtypeStruct(order.shape, order.dtype)),
        [SMEM, HBM, HBM, HBM, HBM],
        [pltpu.VMEM(received.shape, F32), pltpu.SMEM((blocks,), F32), pltpu.SemaphoreType.DMA((5,))],
        8 << 20,
    )(pick, outside(channel), outside(received), outside(noise_var), outside(order))
    take = lax.ppermute(give, "stripe", swap)
    tiles, group = n // TILE, len(planes[0])
    used = tiles * tiles // 2 * TILE + tiles * symbols + tiles // 2
    height = -(-used // group) * group
    part = call(functools.partial(gram, symbols), struct(height, TILE), [VMEM, VMEM])(keep, take)
    part = part.reshape(height, 1, TILE)
    part = lax.all_to_all(part, "stripe", 0, 0, axis_index_groups=planes, tiled=True)
    part = lax.optimization_barrier(part.reshape(height, TILE))
    part = jnp.sum(part.reshape(group, height // group, TILE), axis=0)
    part = lax.optimization_barrier(jnp.broadcast_to(part, (group, *part.shape)).reshape(height, TILE))
    part = part.reshape(height, 1, TILE)
    whole = lax.all_to_all(part, "stripe", 0, 0, axis_index_groups=planes, tiled=True)
    whole = whole.reshape(height, TILE)
    half = jax.ShapeDtypeStruct((n, n), BF16)
    diag, flag, x, e, v = call(
        functools.partial(invert, symbols),
        (struct(1, n), jax.ShapeDtypeStruct((1,), jnp.int32), half, half, half),
        [VMEM],
        [pltpu.VMEM((n, n), F32), pltpu.VMEM((2 * n, n), BF16), pltpu.VMEM((n, n), F32)],
        outs_in=(VMEM, SMEM, VMEM, VMEM, VMEM),
    )(whole)
    rows = call(apply, struct(2 * symbols, n), [SMEM, SMEM] + [VMEM] * 5, flops=10**9)(
        pick, flag, whole, downlink, x, e, v
    )
    other = lax.ppermute(rows, "stripe", swap)
    diag = diag + lax.ppermute(diag, "sub", cores)
    diag = diag + lax.ppermute(diag, ("stripe", "sub"), across)
    diag = diag + lax.ppermute(diag, "stripe", swap)
    transmit, owned = call(
        functools.partial(finish, blocks * subs),
        (struct(blocks, symbols, antennas), struct(blocks, order.shape[1], symbols)),
        [SMEM, VMEM, VMEM, VMEM, VMEM, VMEM],
    )(pick, rows, other, diag, channel, order)
    return transmit, owned.transpose(0, 2, 1)


def solution(mesh):
    return jax.shard_map(
        shards,
        mesh=mesh,
        in_specs=(
            P("sub", "stripe", None, None),
            P("sub", None, "stripe"),
            P("sub", "stripe"),
            P("sub", None, None),
            P("stripe"),
        ),
        out_specs=(P("sub", None, "stripe"), P("sub", None, "stripe")),
        check_vma=False,
    )
```

```python
import functools

import jax
import jax.numpy as jnp
from jax import lax
from jax.experimental import pallas as pl
from jax.experimental.pallas import tpu as pltpu
from jax.sharding import PartitionSpec as P


prior_var = 0.1
TILE = 128
F32, BF16 = jnp.float32, jnp.bfloat16


def mm(left, right, dims=((1,), (0,))):
    return lax.dot_general(left, right, (dims, ((), ())), preferred_element_type=F32)


def exact(left, right):
    return jnp.dot(left, right, precision=lax.Precision.HIGHEST, preferred_element_type=F32)


def split(value):
    high = value.astype(BF16)
    return high, (value - high.astype(F32)).astype(BF16)


def kept_block():
    return lax.bitwise_and(lax.shift_right_logical(lax.axis_index("stripe"), 2), 1)


def enter(channel_ref, received_ref, noise_ref, order_ref, keep_ref, give_ref, kept_ref, samples, noise, sems):
    mine = kept_block()
    antennas = channel_ref.shape[1]
    sides = ((mine, keep_ref), (1 - mine, give_ref))
    copies = [
        pltpu.make_async_copy(received_ref, samples, sems.at[0]),
        pltpu.make_async_copy(noise_ref, noise, sems.at[1]),
        pltpu.make_async_copy(order_ref, kept_ref, sems.at[2]),
    ] + [
        pltpu.make_async_copy(channel_ref.at[which], out_ref.at[pl.ds(0, antennas)], sems.at[3 + k])
        for k, (which, out_ref) in enumerate(sides)
    ]
    for copy in copies:
        copy.start()
    for copy in copies[:2]:
        copy.wait()
    for which, out_ref in sides:
        out_ref[antennas:] = jnp.full((8, out_ref.shape[1]), noise[which], F32)
        for k in range(samples.shape[1] // 8):
            out_ref[antennas:, k * TILE : k * TILE + antennas] = samples[which, 8 * k : 8 * k + 8]
    for copy in copies[2:]:
        copy.wait()


def gram(symbols, keep_ref, take_ref, out_ref):
    antennas, users = keep_ref.shape[0] - 8, keep_ref.shape[1]

    def scaled(ref):
        extra = ref[antennas:]
        scale = 1.0 / jnp.sqrt(extra[:1, antennas : antennas + 1])
        chunks = [extra[:, k * TILE : k * TILE + antennas] for k in range(symbols // 8)]
        return ref[:antennas] * scale, jnp.concatenate(chunks, axis=0) * scale

    own, own_samples = scaled(keep_ref)
    other, other_samples = scaled(take_ref)
    both = jnp.concatenate([own, other], axis=0)
    samples = jnp.concatenate([own_samples, other_samples], axis=1)
    high, low = split(both)
    left = jnp.concatenate([high, high, low], axis=0).T
    right = jnp.concatenate([high, low, high], axis=0)
    y_high, y_low = split(samples)
    mixed = mm(jnp.concatenate([y_high, y_high, y_low], axis=1), right)
    tiles, at = users // TILE, 0
    lower = lower_of(TILE)
    diagonal = []
    for i in range(tiles):
        row = mm(left[i * TILE : (i + 1) * TILE], right[:, : (i + 1) * TILE])
        for j in range(i):
            out_ref[at : at + TILE] = row[:, j * TILE : (j + 1) * TILE]
            at += TILE
        diagonal.append(row[:, i * TILE :])
    for i in range(0, tiles, 2):
        out_ref[at : at + TILE] = jnp.where(lower, diagonal[i], diagonal[i + 1])
        at += TILE
    for j in range(tiles):
        out_ref[at : at + symbols] = mixed[:, j * TILE : (j + 1) * TILE]
        at += symbols
    out_ref[at:] = jnp.zeros((out_ref.shape[0] - at, TILE), F32)
    for i in range(1, tiles, 2):
        out_ref[at : at + 1] = jnp.sum(jnp.where(eye_of(TILE), diagonal[i], 0.0), axis=0, keepdims=True)
        at += 1


def lower_of(n):
    return lax.broadcasted_iota(jnp.int32, (n, n), 0) >= lax.broadcasted_iota(jnp.int32, (n, n), 1)


def eye_of(n):
    return lax.broadcasted_iota(jnp.int32, (n, n), 0) == lax.broadcasted_iota(jnp.int32, (n, n), 1)


def after(bound):
    square = bound * bound
    return square / (2.0 - square)


def gain_of(bound):
    return 2.0 / (2.0 - bound * bound)


def invert(symbols, gram_ref, diag_ref, flag_ref, x_ref, e_ref, v_ref, a_ref, s_ref, t_ref, u_ref, w_ref):
    n = a_ref.shape[0]
    tiles, at = n // TILE, 0
    prior = 1.0 / prior_var
    lower, middle = lower_of(TILE), eye_of(TILE)
    tail = tiles * tiles // 2 * TILE + tiles * symbols

    def put(i, j, tile):
        a_ref[i * TILE : (i + 1) * TILE, j * TILE : (j + 1) * TILE] = tile

    for i in range(tiles):
        for j in range(i):
            tile = gram_ref[at : at + TILE]
            at += TILE
            put(i, j, tile)
            put(j, i, tile.T)
    for i in range(0, tiles, 2):
        tile = gram_ref[at : at + TILE]
        at += TILE
        flip = tile.T
        put(i, i, jnp.where(lower, tile, flip) + jnp.where(middle, prior, 0.0))
        row = gram_ref[tail + i // 2 : tail + i // 2 + 1] + prior
        put(i + 1, i + 1, jnp.where(middle, row, jnp.where(lower, flip, tile)))
    a = a_ref[...]
    eye = jnp.where(eye_of(n), 1.0, 0.0)
    top = jnp.max(jnp.sum(jnp.abs(a), axis=0, keepdims=True), axis=1, keepdims=True) * 1.0001
    alpha = 2.0 / (prior + top)
    start = (top - prior) / (top + prior)
    left = (eye - alpha * a).astype(BF16)
    s_ref[n:] = ((alpha * gain_of(start)) * (eye + left.astype(F32))).astype(BF16)

    def squared(product, bound):
        square = bound * bound
        scale = 1.0 / (2.0 - square)
        return ((2.0 * scale) * product - (square * scale) * eye).astype(BF16)

    s_ref[:n] = squared(mm(left, left), start)
    first = after(start)
    bound, steps = first, jnp.zeros((1, 1), F32)
    for _ in range(10):
        bound = after(bound)
        steps = steps + jnp.where(bound > 0.0125, 1.0, 0.0)
    steps = jnp.max(steps).astype(jnp.int32)

    def step(index, bound):
        both = mm(s_ref[...], s_ref[:n])
        s_ref[n:] = (gain_of(bound) * (s_ref[n:].astype(F32) + both[n:])).astype(BF16)
        s_ref[:n] = squared(both[:n], bound)
        return after(bound)

    bound = lax.fori_loop(0, steps, step, first)
    x = s_ref[n:]
    x = (gain_of(bound) * (x.astype(F32) + mm(x, s_ref[:n]))).astype(BF16)
    x_ref[...] = x
    a_high, a_low = split(a_ref[...])
    parts = mm(jnp.concatenate([a_high, a_low], axis=0), x)
    error = eye - (parts[:n] + parts[n:])
    e = error.astype(BF16)
    e_ref[...] = e
    both = mm(jnp.concatenate([e, x], axis=0), e)
    twice, update = both[:n], both[n:]
    v_ref[...] = twice.astype(BF16)
    diag = jnp.where(eye_of(n), x.astype(F32) + update, 0.0) + (error + twice) * update
    diag_ref[...] = jnp.sum(diag, axis=0, keepdims=True)
    good = jnp.sum(twice * twice) < 3e-5
    flag_ref[0] = good.astype(jnp.int32)

    @pl.when(jnp.logical_not(good))
    def _():
        full(prior, top, start, a_ref, t_ref, u_ref, w_ref, diag_ref, x_ref, e_ref, v_ref)


def full(prior, top, start, a_ref, t_ref, u_ref, w_ref, diag_ref, x_ref, e_ref, v_ref):
    n = a_ref.shape[0]
    tiles = n // TILE

    def over(body):
        def one(index, carry):
            i, j = index // tiles, index % tiles
            rows, columns = (pl.ds(pl.multiple_of(k * TILE, TILE), TILE) for k in (i, j))
            body(rows, columns, jnp.where(eye_of(TILE) & (i == j), 1.0, 0.0))
            return carry

        lax.fori_loop(0, tiles * tiles, one, 0)

    gain = (2.0 / (prior + top)) * gain_of(start)

    def begin(rows, columns, eye):
        t_ref[rows, columns] = gain * (2.0 * eye - (2.0 / (prior + top)) * a_ref[rows, columns])

    over(begin)

    first = after(start)

    def more(index, carry):
        bound = after(carry[0])
        return bound, carry[1] + jnp.where(carry[0] > 1e-3, 1.0, 0.0)

    steps = lax.fori_loop(0, 40, more, (first, jnp.zeros((1, 1), F32)))[1]

    def step(index, bound):
        def residual(rows, columns, eye):
            u_ref[rows, columns] = eye - exact(a_ref[rows, :], t_ref[:, columns])

        def update(rows, columns, eye):
            w_ref[rows, columns] = gain_of(bound) * (t_ref[rows, columns] + exact(t_ref[rows, :], u_ref[:, columns]))

        def back(rows, columns, eye):
            t_ref[rows, columns] = w_ref[rows, columns]

        over(residual)
        over(update)
        over(back)
        return after(bound)

    lax.fori_loop(0, jnp.max(steps).astype(jnp.int32) + 2, step, first)
    diag_ref[...] = jnp.zeros(diag_ref.shape, F32)

    def finish(rows, columns, eye):
        x = t_ref[rows, columns]
        diag_ref[:, columns] = diag_ref[:, columns] + jnp.sum(x * eye, axis=0, keepdims=True)
        x_ref[rows, columns] = x.astype(BF16)
        e_ref[rows, columns], v_ref[rows, columns] = split(x - x.astype(BF16).astype(F32))

    over(finish)


def apply(flag_ref, gram_ref, downlink_ref, x_ref, e_ref, v_ref, rows_ref):
    symbols, n = downlink_ref.shape[1:]
    tiles = n // TILE
    at = tiles * tiles // 2 * TILE
    mixed = jnp.concatenate([gram_ref[at + symbols * j : at + symbols * (j + 1)] for j in range(tiles)], axis=1)
    rows = jnp.concatenate([downlink_ref[kept_block()], mixed], axis=0)
    good = flag_ref[0] == 1

    @pl.when(good)
    def _():
        high, low = split(rows)
        z = mm(jnp.concatenate([high, low], axis=0), x_ref[...])
        z = z[: 2 * symbols] + z[2 * symbols :]
        z = z + mm(z.astype(BF16), e_ref[...])
        rows_ref[...] = z + mm(z.astype(BF16), v_ref[...])

    @pl.when(jnp.logical_not(good))
    def _():
        x = x_ref[...].astype(F32) + (e_ref[...].astype(F32) + v_ref[...].astype(F32))
        rows_ref[...] = exact(rows, x)


def finish(terms, own_ref, other_ref, diag_ref, channel_ref, order_ref, transmit_ref, owned_ref):
    mine = kept_block()
    blocks, symbols = transmit_ref.shape[0], transmit_ref.shape[1]
    mean_error = diag_ref[...] / terms
    scale = lax.rsqrt(mean_error)
    scale = scale * (1.5 - 0.5 * mean_error * scale * scale)
    n = own_ref.shape[1]
    order = order_ref[...]
    pick = (lax.broadcasted_iota(jnp.int32, (n, order.shape[1]), 0) == order).astype(BF16)
    for block in range(blocks):
        z = jnp.where(mine == block, own_ref[...], other_ref[...])
        high, low = split(z[:symbols] * scale)
        h_high, h_low = split(channel_ref[block])
        left = jnp.concatenate([high, low], axis=0)
        one = mm(left, h_high, ((1,), (1,)))
        two = mm(high, h_low, ((1,), (1,)))
        transmit_ref[block] = one[:symbols] + (one[symbols:] + two)
        x = z[symbols:]
        high = x.astype(BF16)
        rest = x - high.astype(F32)
        middle, low = split(rest)
        parts = mm(jnp.concatenate([high, middle, low], axis=0), pick)
        owned_ref[block] = (parts[:symbols] + (parts[symbols : 2 * symbols] + parts[2 * symbols :])).T


VMEM = pl.BlockSpec(memory_space=pltpu.VMEM)
SMEM = pl.BlockSpec(memory_space=pltpu.SMEM)


HBM = pl.BlockSpec(memory_space=pltpu.HBM)


def call(body, outs, in_specs, scratch=(), grant=48 << 20, outs_in=None, flops=None):
    return pl.pallas_call(
        body,
        out_shape=outs,
        in_specs=in_specs,
        out_specs=outs_in or jax.tree.map(lambda _: VMEM, outs),
        cost_estimate=flops and pl.CostEstimate(flops=flops, bytes_accessed=2 << 20, transcendentals=0),
        scratch_shapes=scratch,
        compiler_params=pltpu.CompilerParams(vmem_limit_bytes=grant),
    )


def shards(channel, received, noise_var, downlink, user_order):
    blocks, _, antennas, n = channel.shape
    symbols = received.shape[1]
    channel = channel.reshape(blocks, antennas, n)
    noise_var = noise_var.reshape(blocks)
    order = user_order.reshape(1, -1)
    links, subs = lax.axis_size("stripe"), lax.axis_size("sub")
    pair, ring = 4, links // 8
    planes = [[x * 8 + y * pair + z for x in range(ring) for z in range(pair)] for y in range(2)]
    swap = [(i, i ^ pair) for i in range(links)]
    cores = [(i, i ^ 1) for i in range(subs)]
    across = [(i * subs + s, (i ^ pair) * subs + (s ^ 2)) for i in range(links) for s in range(subs)]

    def struct(*shape):
        return jax.ShapeDtypeStruct(shape, F32)

    def outside(value):
        return pltpu.with_memory_space_constraint(value, pltpu.HBM)

    keep, give, order = call(
        enter,
        (struct(antennas + 8, n), struct(antennas + 8, n), jax.ShapeDtypeStruct(order.shape, order.dtype)),
        [HBM] * 4,
        [pltpu.VMEM(received.shape, F32), pltpu.SMEM((blocks,), F32), pltpu.SemaphoreType.DMA((5,))],
        8 << 20,
    )(outside(channel), outside(received), outside(noise_var), outside(order))
    take = lax.ppermute(give, "stripe", swap)
    tiles, group = n // TILE, len(planes[0])
    used = tiles * tiles // 2 * TILE + tiles * symbols + tiles // 2
    height = -(-used // group) * group
    part = call(functools.partial(gram, symbols), struct(height, TILE), [VMEM, VMEM])(keep, take)
    part = part.reshape(height, 1, TILE)
    part = lax.all_to_all(part, "stripe", 0, 0, axis_index_groups=planes, tiled=True)
    part = lax.optimization_barrier(part.reshape(height, TILE))
    part = jnp.sum(part.reshape(group, height // group, TILE), axis=0)
    part = lax.optimization_barrier(jnp.broadcast_to(part, (group, *part.shape)).reshape(height, TILE))
    part = part.reshape(height, 1, TILE)
    whole = lax.all_to_all(part, "stripe", 0, 0, axis_index_groups=planes, tiled=True)
    whole = whole.reshape(height, TILE)
    half = jax.ShapeDtypeStruct((n, n), BF16)
    diag, flag, x, e, v = call(
        functools.partial(invert, symbols),
        (struct(1, n), jax.ShapeDtypeStruct((1,), jnp.int32), half, half, half),
        [VMEM],
        [pltpu.VMEM((n, n), F32), pltpu.VMEM((2 * n, n), BF16)] + [pltpu.VMEM((n, n), F32)] * 3,
        outs_in=(VMEM, SMEM, VMEM, VMEM, VMEM),
    )(whole)
    rows = call(apply, struct(2 * symbols, n), [SMEM] + [VMEM] * 5, flops=10**9)(flag, whole, downlink, x, e, v)
    other = lax.ppermute(rows, "stripe", swap)
    diag = diag + lax.ppermute(diag, "sub", cores)
    diag = diag + lax.ppermute(diag, ("stripe", "sub"), across)
    diag = diag + lax.ppermute(diag, "stripe", swap)
    transmit, owned = call(
        functools.partial(finish, blocks * subs),
        (struct(blocks, symbols, antennas), struct(blocks, order.shape[1], symbols)),
        [VMEM] * 5,
    )(rows, other, diag, channel, order)
    return transmit, owned.transpose(0, 2, 1)


def solution(mesh):
    return jax.shard_map(
        shards,
        mesh=mesh,
        in_specs=(
            P("sub", "stripe", None, None),
            P("sub", None, "stripe"),
            P("sub", "stripe"),
            P("sub", None, None),
            P("stripe"),
        ),
        out_specs=(P("sub", None, "stripe"), P("sub", None, "stripe")),
        check_vma=False,
    )
```

```python
import functools

import jax
import jax.numpy as jnp
from jax import lax
from jax.experimental import pallas as pl
from jax.experimental.pallas import tpu as pltpu
from jax.sharding import PartitionSpec as P


prior_var = 0.1
TILE = 128
F32, BF16 = jnp.float32, jnp.bfloat16


def mm(left, right, dims=((1,), (0,))):
    return lax.dot_general(left, right, (dims, ((), ())), preferred_element_type=F32)


def exact(left, right):
    return jnp.dot(left, right, precision=lax.Precision.HIGHEST, preferred_element_type=F32)


def split(value):
    high = value.astype(BF16)
    return high, (value - high.astype(F32)).astype(BF16)


def kept_block():
    return lax.bitwise_and(lax.shift_right_logical(lax.axis_index("stripe"), 2), 1)


def enter(channel_ref, received_ref, noise_ref, order_ref, keep_ref, give_ref, kept_ref, samples, noise, sems):
    mine = kept_block()
    antennas = channel_ref.shape[1]
    sides = ((mine, keep_ref), (1 - mine, give_ref))
    copies = [
        pltpu.make_async_copy(received_ref, samples, sems.at[0]),
        pltpu.make_async_copy(noise_ref, noise, sems.at[1]),
        pltpu.make_async_copy(order_ref, kept_ref, sems.at[2]),
    ] + [
        pltpu.make_async_copy(channel_ref.at[which], out_ref.at[pl.ds(0, antennas)], sems.at[3 + k])
        for k, (which, out_ref) in enumerate(sides)
    ]
    for copy in copies:
        copy.start()
    for copy in copies[:2]:
        copy.wait()
    for which, out_ref in sides:
        out_ref[antennas:] = jnp.full((8, out_ref.shape[1]), noise[which], F32)
        for k in range(samples.shape[1] // 8):
            out_ref[antennas:, k * TILE : k * TILE + antennas] = samples[which, 8 * k : 8 * k + 8]
    for copy in copies[2:]:
        copy.wait()


def gram(symbols, block_ref, *rest):
    *base, out_ref = rest
    antennas, users = block_ref.shape[0] - 8, block_ref.shape[1]

    def put(at, value):
        rows = slice(at, at + value.shape[0])
        out_ref[rows] = base[0][rows] + value if base else value

    extra = block_ref[antennas:]
    scale = 1.0 / jnp.sqrt(extra[:1, antennas : antennas + 1])
    samples = jnp.concatenate([extra[:, k * TILE : k * TILE + antennas] for k in range(symbols // 8)], axis=0)
    high, low = split(block_ref[:antennas] * scale)
    left = jnp.concatenate([high, high, low], axis=0).T
    right = jnp.concatenate([high, low, high], axis=0)
    y_high, y_low = split(samples * scale)
    mixed = mm(jnp.concatenate([y_high, y_high, y_low], axis=1), right)
    tiles, at = users // TILE, 0
    lower = lower_of(TILE)
    diagonal = []
    for i in range(tiles):
        row = mm(left[i * TILE : (i + 1) * TILE], right[:, : (i + 1) * TILE])
        for j in range(i):
            put(at, row[:, j * TILE : (j + 1) * TILE])
            at += TILE
        diagonal.append(row[:, i * TILE :])
    for i in range(0, tiles, 2):
        put(at, jnp.where(lower, diagonal[i], diagonal[i + 1]))
        at += TILE
    for j in range(tiles):
        put(at, mixed[:, j * TILE : (j + 1) * TILE])
        at += symbols
    ends = [
        jnp.sum(jnp.where(eye_of(TILE), diagonal[i], 0.0), axis=0, keepdims=True) for i in range(1, tiles, 2)
    ]
    put(at, jnp.concatenate(ends + [jnp.zeros((out_ref.shape[0] - at - len(ends), TILE), F32)], axis=0))


def lower_of(n):
    return lax.broadcasted_iota(jnp.int32, (n, n), 0) >= lax.broadcasted_iota(jnp.int32, (n, n), 1)


def eye_of(n):
    return lax.broadcasted_iota(jnp.int32, (n, n), 0) == lax.broadcasted_iota(jnp.int32, (n, n), 1)


def after(bound):
    square = bound * bound
    return square / (2.0 - square)


def gain_of(bound):
    return 2.0 / (2.0 - bound * bound)


def invert(symbols, gram_ref, diag_ref, flag_ref, x_ref, e_ref, v_ref, a_ref, s_ref, t_ref, u_ref, w_ref):
    n = a_ref.shape[0]
    tiles, at = n // TILE, 0
    prior = 1.0 / prior_var
    lower, middle = lower_of(TILE), eye_of(TILE)
    tail = tiles * tiles // 2 * TILE + tiles * symbols

    def put(i, j, tile):
        a_ref[i * TILE : (i + 1) * TILE, j * TILE : (j + 1) * TILE] = tile

    for i in range(tiles):
        for j in range(i):
            tile = gram_ref[at : at + TILE]
            at += TILE
            put(i, j, tile)
            put(j, i, tile.T)
    for i in range(0, tiles, 2):
        tile = gram_ref[at : at + TILE]
        at += TILE
        flip = tile.T
        put(i, i, jnp.where(lower, tile, flip) + jnp.where(middle, prior, 0.0))
        row = gram_ref[tail + i // 2 : tail + i // 2 + 1] + prior
        put(i + 1, i + 1, jnp.where(middle, row, jnp.where(lower, flip, tile)))
    a = a_ref[...]
    eye = jnp.where(eye_of(n), 1.0, 0.0)
    top = jnp.max(jnp.sum(jnp.abs(a), axis=0, keepdims=True), axis=1, keepdims=True) * 1.0001
    alpha = 2.0 / (prior + top)
    start = (top - prior) / (top + prior)
    left = (eye - alpha * a).astype(BF16)
    s_ref[n:] = ((alpha * gain_of(start)) * (eye + left.astype(F32))).astype(BF16)

    def squared(product, bound):
        square = bound * bound
        scale = 1.0 / (2.0 - square)
        return ((2.0 * scale) * product - (square * scale) * eye).astype(BF16)

    s_ref[:n] = squared(mm(left, left), start)
    first = after(start)
    bound, steps = first, jnp.zeros((1, 1), F32)
    for _ in range(10):
        bound = after(bound)
        steps = steps + jnp.where(bound > 0.0125, 1.0, 0.0)
    steps = jnp.max(steps).astype(jnp.int32)

    def step(index, bound):
        both = mm(s_ref[...], s_ref[:n])
        s_ref[n:] = (gain_of(bound) * (s_ref[n:].astype(F32) + both[n:])).astype(BF16)
        s_ref[:n] = squared(both[:n], bound)
        return after(bound)

    bound = lax.fori_loop(0, steps, step, first)
    x = s_ref[n:]
    x = (gain_of(bound) * (x.astype(F32) + mm(x, s_ref[:n]))).astype(BF16)
    x_ref[...] = x
    a_high, a_low = split(a_ref[...])
    strips = [slice(at, at + 128) for at in range(0, n, 128)]
    parts = mm(jnp.concatenate([part for rows in strips for part in (a_high[rows], a_low[rows])], axis=0), x)
    for k, rows in enumerate(strips):
        product = parts[2 * k * 128 : (2 * k + 1) * 128] + parts[(2 * k + 1) * 128 : (2 * k + 2) * 128]
        e_ref[rows] = (eye[rows] - product).astype(BF16)
    e = e_ref[...]
    blocks = [slice(at, at + 128) for at in range(0, n, 128)]
    both = mm(jnp.concatenate([part for rows in blocks for part in (e[rows], x[rows])], axis=0), e)
    diag, size = jnp.zeros((1, n), F32), jnp.zeros((1, n), F32)
    for k, rows in enumerate(blocks):
        twice = both[2 * k * 128 : (2 * k + 1) * 128]
        update = both[(2 * k + 1) * 128 : (2 * k + 2) * 128]
        v_ref[rows] = twice.astype(BF16)
        own = jnp.where(eye[rows] > 0.0, x[rows].astype(F32) + update, 0.0)
        diag = diag + jnp.sum(own + (e[rows].astype(F32) + twice) * update, axis=0, keepdims=True)
        size = size + jnp.sum(twice * twice, axis=0, keepdims=True)
    diag_ref[...] = diag
    good = jnp.sum(size) < 3e-5
    flag_ref[0] = good.astype(jnp.int32)

    @pl.when(jnp.logical_not(good))
    def _():
        full(prior, top, start, a_ref, t_ref, u_ref, w_ref, diag_ref, x_ref, e_ref, v_ref)


def full(prior, top, start, a_ref, t_ref, u_ref, w_ref, diag_ref, x_ref, e_ref, v_ref):
    n = a_ref.shape[0]
    tiles = n // TILE

    def over(body):
        def one(index, carry):
            i, j = index // tiles, index % tiles
            rows, columns = (pl.ds(pl.multiple_of(k * TILE, TILE), TILE) for k in (i, j))
            body(rows, columns, jnp.where(eye_of(TILE) & (i == j), 1.0, 0.0))
            return carry

        lax.fori_loop(0, tiles * tiles, one, 0)

    gain = (2.0 / (prior + top)) * gain_of(start)

    def begin(rows, columns, eye):
        t_ref[rows, columns] = gain * (2.0 * eye - (2.0 / (prior + top)) * a_ref[rows, columns])

    over(begin)

    first = after(start)

    def more(index, carry):
        bound = after(carry[0])
        return bound, carry[1] + jnp.where(carry[0] > 1e-3, 1.0, 0.0)

    steps = lax.fori_loop(0, 40, more, (first, jnp.zeros((1, 1), F32)))[1]

    def step(index, bound):
        def residual(rows, columns, eye):
            u_ref[rows, columns] = eye - exact(a_ref[rows, :], t_ref[:, columns])

        def update(rows, columns, eye):
            w_ref[rows, columns] = gain_of(bound) * (t_ref[rows, columns] + exact(t_ref[rows, :], u_ref[:, columns]))

        def back(rows, columns, eye):
            t_ref[rows, columns] = w_ref[rows, columns]

        over(residual)
        over(update)
        over(back)
        return after(bound)

    lax.fori_loop(0, jnp.max(steps).astype(jnp.int32) + 2, step, first)
    diag_ref[...] = jnp.zeros(diag_ref.shape, F32)

    def finish(rows, columns, eye):
        x = t_ref[rows, columns]
        diag_ref[:, columns] = diag_ref[:, columns] + jnp.sum(x * eye, axis=0, keepdims=True)
        x_ref[rows, columns] = x.astype(BF16)
        e_ref[rows, columns], v_ref[rows, columns] = split(x - x.astype(BF16).astype(F32))

    over(finish)


def apply(flag_ref, gram_ref, downlink_ref, x_ref, e_ref, v_ref, rows_ref):
    symbols, n = downlink_ref.shape[1:]
    tiles = n // TILE
    at = tiles * tiles // 2 * TILE
    mixed = jnp.concatenate([gram_ref[at + symbols * j : at + symbols * (j + 1)] for j in range(tiles)], axis=1)
    rows = jnp.concatenate([downlink_ref[kept_block()], mixed], axis=0)
    good = flag_ref[0] == 1

    @pl.when(good)
    def _():
        high, low = split(rows)
        z = mm(jnp.concatenate([high, low], axis=0), x_ref[...])
        z = z[: 2 * symbols] + z[2 * symbols :]
        z = z + mm(z.astype(BF16), e_ref[...])
        rows_ref[...] = z + mm(z.astype(BF16), v_ref[...])

    @pl.when(jnp.logical_not(good))
    def _():
        x = x_ref[...].astype(F32) + (e_ref[...].astype(F32) + v_ref[...].astype(F32))
        rows_ref[...] = exact(rows, x)


def finish(terms, own_ref, other_ref, diag_ref, channel_ref, order_ref, transmit_ref, owned_ref):
    mine = kept_block()
    blocks, symbols = transmit_ref.shape[0], transmit_ref.shape[1]
    mean_error = diag_ref[...] / terms
    scale = lax.rsqrt(mean_error)
    scale = scale * (1.5 - 0.5 * mean_error * scale * scale)
    n = own_ref.shape[1]
    order = order_ref[...]
    pick = (lax.broadcasted_iota(jnp.int32, (n, order.shape[1]), 0) == order).astype(BF16)
    for block in range(blocks):
        z = jnp.where(mine == block, own_ref[...], other_ref[...])
        high, low = split(z[:symbols] * scale)
        h_high, h_low = split(channel_ref[block])
        left = jnp.concatenate([high, low], axis=0)
        one = mm(left, h_high, ((1,), (1,)))
        two = mm(high, h_low, ((1,), (1,)))
        transmit_ref[block] = one[:symbols] + (one[symbols:] + two)
        x = z[symbols:]
        high = x.astype(BF16)
        rest = x - high.astype(F32)
        middle, low = split(rest)
        parts = mm(jnp.concatenate([high, middle, low], axis=0), pick)
        owned_ref[block] = (parts[:symbols] + (parts[symbols : 2 * symbols] + parts[2 * symbols :])).T


VMEM = pl.BlockSpec(memory_space=pltpu.VMEM)
SMEM = pl.BlockSpec(memory_space=pltpu.SMEM)


HBM = pl.BlockSpec(memory_space=pltpu.HBM)


def call(body, outs, in_specs, scratch=(), grant=48 << 20, outs_in=None, flops=None):
    return pl.pallas_call(
        body,
        out_shape=outs,
        in_specs=in_specs,
        out_specs=outs_in or jax.tree.map(lambda _: VMEM, outs),
        cost_estimate=flops and pl.CostEstimate(flops=flops, bytes_accessed=2 << 20, transcendentals=0),
        scratch_shapes=scratch,
        compiler_params=pltpu.CompilerParams(vmem_limit_bytes=grant),
    )


def shards(channel, received, noise_var, downlink, user_order):
    blocks, _, antennas, n = channel.shape
    symbols = received.shape[1]
    channel = channel.reshape(blocks, antennas, n)
    noise_var = noise_var.reshape(blocks)
    order = user_order.reshape(1, -1)
    links, subs = lax.axis_size("stripe"), lax.axis_size("sub")
    pair, ring = 4, links // 8
    planes = [[x * 8 + y * pair + z for x in range(ring) for z in range(pair)] for y in range(2)]
    swap = [(i, i ^ pair) for i in range(links)]
    cores = [(i, i ^ 1) for i in range(subs)]
    across = [(i * subs + s, (i ^ pair) * subs + (s ^ 2)) for i in range(links) for s in range(subs)]

    def struct(*shape):
        return jax.ShapeDtypeStruct(shape, F32)

    def outside(value):
        return pltpu.with_memory_space_constraint(value, pltpu.HBM)

    keep, give, order = call(
        enter,
        (struct(antennas + 8, n), struct(antennas + 8, n), jax.ShapeDtypeStruct(order.shape, order.dtype)),
        [HBM] * 4,
        [pltpu.VMEM(received.shape, F32), pltpu.SMEM((blocks,), F32), pltpu.SemaphoreType.DMA((5,))],
        8 << 20,
    )(outside(channel), outside(received), outside(noise_var), outside(order))
    tiles, group = n // TILE, len(planes[0])
    used = tiles * tiles // 2 * TILE + tiles * symbols + tiles // 2
    height = -(-used // group) * group
    take = lax.ppermute(give, "stripe", swap)
    own = call(functools.partial(gram, symbols), struct(height, TILE), [VMEM], flops=10**9)(keep)
    part = call(functools.partial(gram, symbols), struct(height, TILE), [VMEM, VMEM])(take, own)
    part = part.reshape(height, 1, TILE)
    part = lax.all_to_all(part, "stripe", 0, 0, axis_index_groups=planes, tiled=True)
    part = lax.optimization_barrier(part.reshape(height, TILE))
    part = jnp.sum(part.reshape(group, height // group, TILE), axis=0)
    part = lax.optimization_barrier(jnp.broadcast_to(part, (group, *part.shape)).reshape(height, TILE))
    part = part.reshape(height, 1, TILE)
    whole = lax.all_to_all(part, "stripe", 0, 0, axis_index_groups=planes, tiled=True)
    whole = whole.reshape(height, TILE)
    half = jax.ShapeDtypeStruct((n, n), BF16)
    diag, flag, x, e, v = call(
        functools.partial(invert, symbols),
        (struct(1, n), jax.ShapeDtypeStruct((1,), jnp.int32), half, half, half),
        [VMEM],
        [pltpu.VMEM((n, n), F32), pltpu.VMEM((2 * n, n), BF16)] + [pltpu.VMEM((n, n), F32)] * 3,
        outs_in=(VMEM, SMEM, VMEM, VMEM, VMEM),
    )(whole)
    rows = call(apply, struct(2 * symbols, n), [SMEM] + [VMEM] * 5, flops=10**9)(flag, whole, downlink, x, e, v)
    other = lax.ppermute(rows, "stripe", swap)
    diag = diag + lax.ppermute(diag, "sub", cores)
    diag = diag + lax.ppermute(diag, ("stripe", "sub"), across)
    diag = diag + lax.ppermute(diag, "stripe", swap)
    transmit, owned = call(
        functools.partial(finish, blocks * subs),
        (struct(blocks, symbols, antennas), struct(blocks, order.shape[1], symbols)),
        [VMEM] * 5,
    )(rows, other, diag, channel, order)
    return transmit, owned.transpose(0, 2, 1)


def solution(mesh):
    return jax.shard_map(
        shards,
        mesh=mesh,
        in_specs=(
            P("sub", "stripe", None, None),
            P("sub", None, "stripe"),
            P("sub", "stripe"),
            P("sub", None, None),
            P("stripe"),
        ),
        out_specs=(P("sub", None, "stripe"), P("sub", None, "stripe")),
        check_vma=False,
    )
```

```python
import functools

import jax
import jax.numpy as jnp
from jax import lax
from jax.experimental import pallas as pl
from jax.experimental.pallas import tpu as pltpu
from jax.sharding import PartitionSpec as P


prior_var = 0.1
TILE = 128
F32, BF16 = jnp.float32, jnp.bfloat16


def mm(left, right, dims=((1,), (0,))):
    return lax.dot_general(left, right, (dims, ((), ())), preferred_element_type=F32)


def exact(left, right):
    return jnp.dot(left, right, precision=lax.Precision.HIGHEST, preferred_element_type=F32)


def split(value):
    high = value.astype(BF16)
    return high, (value - high.astype(F32)).astype(BF16)


def kept_block():
    return lax.bitwise_and(lax.shift_right_logical(lax.axis_index("stripe"), 2), 1)


def enter(channel_ref, received_ref, noise_ref, order_ref, keep_ref, give_ref, kept_ref, samples, noise, sems):
    mine = kept_block()
    antennas = channel_ref.shape[1]
    sides = ((mine, keep_ref), (1 - mine, give_ref))
    copies = [
        pltpu.make_async_copy(received_ref, samples, sems.at[0]),
        pltpu.make_async_copy(noise_ref, noise, sems.at[1]),
        pltpu.make_async_copy(order_ref, kept_ref, sems.at[2]),
    ] + [
        pltpu.make_async_copy(channel_ref.at[which], out_ref.at[pl.ds(0, antennas)], sems.at[3 + k])
        for k, (which, out_ref) in enumerate(sides)
    ]
    for copy in copies:
        copy.start()
    for copy in copies[:3]:
        copy.wait()
    for which, out_ref in sides:
        out_ref[antennas:] = jnp.full((8, out_ref.shape[1]), noise[which], F32)
        for k in range(samples.shape[1] // 8):
            out_ref[antennas:, k * TILE : k * TILE + antennas] = samples[which, 8 * k : 8 * k + 8]
    give_ref[antennas : antennas + 1, order_lanes(antennas, order_ref.shape[1])] = kept_ref[...].astype(F32)
    for copy in copies[3:]:
        copy.wait()


def order_lanes(antennas, count):
    return slice(TILE + antennas, TILE + antennas + count)


def gram(symbols, block_ref, *rest):
    *base, out_ref = rest
    antennas, users = block_ref.shape[0] - 8, block_ref.shape[1]

    def put(at, value):
        rows = slice(at, at + value.shape[0])
        out_ref[rows] = base[0][rows] + value if base else value

    extra = block_ref[antennas:]
    scale = 1.0 / jnp.sqrt(extra[:1, antennas : antennas + 1])
    samples = jnp.concatenate([extra[:, k * TILE : k * TILE + antennas] for k in range(symbols // 8)], axis=0)
    high, low = split(block_ref[:antennas] * scale)
    left = jnp.concatenate([high, high, low], axis=0).T
    right = jnp.concatenate([high, low, high], axis=0)
    y_high, y_low = split(samples * scale)
    mixed = mm(jnp.concatenate([y_high, y_high, y_low], axis=1), right)
    tiles, at = users // TILE, 0
    lower = lower_of(TILE)
    diagonal = []
    for i in range(tiles):
        row = mm(left[i * TILE : (i + 1) * TILE], right[:, : (i + 1) * TILE])
        for j in range(i):
            put(at, row[:, j * TILE : (j + 1) * TILE])
            at += TILE
        diagonal.append(row[:, i * TILE :])
    for i in range(0, tiles, 2):
        put(at, jnp.where(lower, diagonal[i], diagonal[i + 1]))
        at += TILE
    for j in range(tiles):
        put(at, mixed[:, j * TILE : (j + 1) * TILE])
        at += symbols
    ends = [
        jnp.sum(jnp.where(eye_of(TILE), diagonal[i], 0.0), axis=0, keepdims=True) for i in range(1, tiles, 2)
    ]
    put(at, jnp.concatenate(ends + [jnp.zeros((out_ref.shape[0] - at - len(ends), TILE), F32)], axis=0))


def lower_of(n):
    return lax.broadcasted_iota(jnp.int32, (n, n), 0) >= lax.broadcasted_iota(jnp.int32, (n, n), 1)


def eye_of(n):
    return lax.broadcasted_iota(jnp.int32, (n, n), 0) == lax.broadcasted_iota(jnp.int32, (n, n), 1)


def after(bound):
    square = bound * bound
    return square / (2.0 - square)


def gain_of(bound):
    return 2.0 / (2.0 - bound * bound)


def invert(symbols, gram_ref, diag_ref, flag_ref, x_ref, e_ref, v_ref, a_ref, s_ref, t_ref, u_ref, w_ref):
    n = a_ref.shape[0]
    tiles, at = n // TILE, 0
    prior = 1.0 / prior_var
    lower, middle = lower_of(TILE), eye_of(TILE)
    tail = tiles * tiles // 2 * TILE + tiles * symbols

    def put(i, j, tile):
        a_ref[i * TILE : (i + 1) * TILE, j * TILE : (j + 1) * TILE] = tile

    for i in range(tiles):
        for j in range(i):
            tile = gram_ref[at : at + TILE]
            at += TILE
            put(i, j, tile)
            put(j, i, tile.T)
    for i in range(0, tiles, 2):
        tile = gram_ref[at : at + TILE]
        at += TILE
        flip = tile.T
        put(i, i, jnp.where(lower, tile, flip) + jnp.where(middle, prior, 0.0))
        row = gram_ref[tail + i // 2 : tail + i // 2 + 1] + prior
        put(i + 1, i + 1, jnp.where(middle, row, jnp.where(lower, flip, tile)))
    a = a_ref[...]
    eye = jnp.where(eye_of(n), 1.0, 0.0)
    top = jnp.max(jnp.sum(jnp.abs(a), axis=0, keepdims=True), axis=1, keepdims=True) * 1.0001
    alpha = 2.0 / (prior + top)
    start = (top - prior) / (top + prior)
    a_high, a_low = split(a)
    rounded = a_high.astype(F32)
    gain = alpha * gain_of(start)
    s_ref[n:] = ((2.0 * gain) * eye - (gain * alpha) * rounded).astype(BF16)

    def squared(product, bound):
        square = bound * bound
        scale = 1.0 / (2.0 - square)
        return ((2.0 * scale) * product - (square * scale) * eye).astype(BF16)

    scale = 2.0 * alpha / (2.0 - start * start)
    s_ref[:n] = (eye + (scale * alpha) * mm(a_high, a_high) - (2.0 * scale) * rounded).astype(BF16)
    first = after(start)
    bound, steps = first, jnp.zeros((1, 1), F32)
    for _ in range(10):
        bound = after(bound)
        steps = steps + jnp.where(bound > 0.0125, 1.0, 0.0)
    steps = jnp.max(steps).astype(jnp.int32)

    def step(index, bound):
        both = mm(s_ref[...], s_ref[:n])
        s_ref[n:] = (gain_of(bound) * (s_ref[n:].astype(F32) + both[n:])).astype(BF16)
        s_ref[:n] = squared(both[:n], bound)
        return after(bound)

    bound = lax.fori_loop(0, steps, step, first)
    x = s_ref[n:]
    x = (gain_of(bound) * (x.astype(F32) + mm(x, s_ref[:n]))).astype(BF16)
    x_ref[...] = x
    strips = [slice(at, at + 128) for at in range(0, n, 128)]
    parts = mm(jnp.concatenate([part for rows in strips for part in (a_high[rows], a_low[rows])], axis=0), x)
    for k, rows in enumerate(strips):
        product = parts[2 * k * 128 : (2 * k + 1) * 128] + parts[(2 * k + 1) * 128 : (2 * k + 2) * 128]
        e_ref[rows] = (eye[rows] - product).astype(BF16)
    e = e_ref[...]
    blocks = [slice(at, at + 128) for at in range(0, n, 128)]
    both = mm(jnp.concatenate([part for rows in blocks for part in (e[rows], x[rows])], axis=0), e)
    diag, size = jnp.zeros((1, n), F32), jnp.zeros((1, n), F32)
    for k, rows in enumerate(blocks):
        twice = both[2 * k * 128 : (2 * k + 1) * 128]
        update = both[(2 * k + 1) * 128 : (2 * k + 2) * 128]
        v_ref[rows] = twice.astype(BF16)
        own = jnp.where(eye[rows] > 0.0, x[rows].astype(F32) + update, 0.0)
        diag = diag + jnp.sum(own + (e[rows].astype(F32) + twice) * update, axis=0, keepdims=True)
        size = size + jnp.sum(twice * twice, axis=0, keepdims=True)
    diag_ref[...] = diag
    good = jnp.sum(size) < 3e-5
    flag_ref[0] = good.astype(jnp.int32)

    @pl.when(jnp.logical_not(good))
    def _():
        full(prior, top, start, a_ref, t_ref, u_ref, w_ref, diag_ref, x_ref, e_ref, v_ref)


def full(prior, top, start, a_ref, t_ref, u_ref, w_ref, diag_ref, x_ref, e_ref, v_ref):
    n = a_ref.shape[0]
    tiles = n // TILE

    def over(body):
        def one(index, carry):
            i, j = index // tiles, index % tiles
            rows, columns = (pl.ds(pl.multiple_of(k * TILE, TILE), TILE) for k in (i, j))
            body(rows, columns, jnp.where(eye_of(TILE) & (i == j), 1.0, 0.0))
            return carry

        lax.fori_loop(0, tiles * tiles, one, 0)

    gain = (2.0 / (prior + top)) * gain_of(start)

    def begin(rows, columns, eye):
        t_ref[rows, columns] = gain * (2.0 * eye - (2.0 / (prior + top)) * a_ref[rows, columns])

    over(begin)

    first = after(start)

    def more(index, carry):
        bound = after(carry[0])
        return bound, carry[1] + jnp.where(carry[0] > 1e-3, 1.0, 0.0)

    steps = lax.fori_loop(0, 40, more, (first, jnp.zeros((1, 1), F32)))[1]

    def step(index, bound):
        def residual(rows, columns, eye):
            u_ref[rows, columns] = eye - exact(a_ref[rows, :], t_ref[:, columns])

        def update(rows, columns, eye):
            w_ref[rows, columns] = gain_of(bound) * (t_ref[rows, columns] + exact(t_ref[rows, :], u_ref[:, columns]))

        def back(rows, columns, eye):
            t_ref[rows, columns] = w_ref[rows, columns]

        over(residual)
        over(update)
        over(back)
        return after(bound)

    lax.fori_loop(0, jnp.max(steps).astype(jnp.int32) + 2, step, first)
    diag_ref[...] = jnp.zeros(diag_ref.shape, F32)

    def finish(rows, columns, eye):
        x = t_ref[rows, columns]
        diag_ref[:, columns] = diag_ref[:, columns] + jnp.sum(x * eye, axis=0, keepdims=True)
        x_ref[rows, columns] = x.astype(BF16)
        e_ref[rows, columns], v_ref[rows, columns] = split(x - x.astype(BF16).astype(F32))

    over(finish)


def apply(flag_ref, gram_ref, downlink_ref, x_ref, e_ref, v_ref, rows_ref):
    symbols, n = downlink_ref.shape[1:]
    tiles = n // TILE
    at = tiles * tiles // 2 * TILE
    mixed = jnp.concatenate([gram_ref[at + symbols * j : at + symbols * (j + 1)] for j in range(tiles)], axis=1)
    rows = jnp.concatenate([downlink_ref[kept_block()], mixed], axis=0)
    good = flag_ref[0] == 1

    @pl.when(good)
    def _():
        high, low = split(rows)
        z = mm(jnp.concatenate([high, low], axis=0), x_ref[...])
        z = z[: 2 * symbols] + z[2 * symbols :]
        z = z + mm(z.astype(BF16), e_ref[...])
        rows_ref[...] = z + mm(z.astype(BF16), v_ref[...])

    @pl.when(jnp.logical_not(good))
    def _():
        x = x_ref[...].astype(F32) + (e_ref[...].astype(F32) + v_ref[...].astype(F32))
        rows_ref[...] = exact(rows, x)


def claim(symbols, rows_ref, order_ref, take_ref, give_ref, owned_ref):
    n, count = rows_ref.shape[1], order_ref.shape[1]
    antennas = take_ref.shape[0] - 8
    theirs = take_ref[antennas : antennas + 1, order_lanes(antennas, count)].astype(jnp.int32)
    order = jnp.concatenate([order_ref[...], theirs], axis=1)
    pick = (lax.broadcasted_iota(jnp.int32, (n, 2 * count), 0) == order).astype(BF16)
    x = rows_ref[symbols:]
    high = x.astype(BF16)
    middle, low = split(x - high.astype(F32))
    parts = mm(jnp.concatenate([high, middle, low], axis=0), pick)
    picked = (parts[:symbols] + (parts[symbols : 2 * symbols] + parts[2 * symbols :])).T
    owned_ref[...] = picked[:count]
    give_ref[:symbols] = rows_ref[:symbols]
    give_ref[symbols:] = jnp.zeros((8, n), F32)
    for k in range(count // 8):
        give_ref[symbols:, k * TILE : k * TILE + symbols] = picked[count + 8 * k : count + 8 * k + 8]


def finish(terms, own_ref, other_ref, mine_ref, diag_ref, channel_ref, transmit_ref, owned_ref):
    mine = kept_block()
    symbols, count = transmit_ref.shape[1], owned_ref.shape[1]
    mean_error = diag_ref[...] / terms
    scale = lax.rsqrt(mean_error)
    scale = scale * (1.5 - 0.5 * mean_error * scale * scale)
    for block, rows_ref in ((mine, own_ref), (1 - mine, other_ref)):
        high, low = split(rows_ref[:symbols] * scale)
        h_high, h_low = split(channel_ref[block])
        left = jnp.concatenate([high, low], axis=0)
        one = mm(left, h_high, ((1,), (1,)))
        two = mm(high, h_low, ((1,), (1,)))
        transmit_ref[block] = one[:symbols] + (one[symbols:] + two)
    owned_ref[mine] = mine_ref[...]
    theirs = [other_ref[symbols:, k * TILE : k * TILE + symbols] for k in range(count // 8)]
    owned_ref[1 - mine] = jnp.concatenate(theirs, axis=0)


VMEM = pl.BlockSpec(memory_space=pltpu.VMEM)
SMEM = pl.BlockSpec(memory_space=pltpu.SMEM)


HBM = pl.BlockSpec(memory_space=pltpu.HBM)


def call(body, outs, in_specs, scratch=(), grant=48 << 20, outs_in=None, flops=None):
    return pl.pallas_call(
        body,
        out_shape=outs,
        in_specs=in_specs,
        out_specs=outs_in or jax.tree.map(lambda _: VMEM, outs),
        cost_estimate=flops and pl.CostEstimate(flops=flops, bytes_accessed=2 << 20, transcendentals=0),
        scratch_shapes=scratch,
        compiler_params=pltpu.CompilerParams(vmem_limit_bytes=grant),
    )


def shards(channel, received, noise_var, downlink, user_order):
    blocks, _, antennas, n = channel.shape
    symbols = received.shape[1]
    channel = channel.reshape(blocks, antennas, n)
    noise_var = noise_var.reshape(blocks)
    order = user_order.reshape(1, -1)
    links, subs = lax.axis_size("stripe"), lax.axis_size("sub")
    pair, ring = 4, links // 8
    planes = [[x * 8 + y * pair + z for x in range(ring) for z in range(pair)] for y in range(2)]
    swap = [(i, i ^ pair) for i in range(links)]
    cores = [(i, i ^ 1) for i in range(subs)]
    across = [(i * subs + s, (i ^ pair) * subs + (s ^ 2)) for i in range(links) for s in range(subs)]

    def struct(*shape):
        return jax.ShapeDtypeStruct(shape, F32)

    def outside(value):
        return pltpu.with_memory_space_constraint(value, pltpu.HBM)

    keep, give, order = call(
        enter,
        (struct(antennas + 8, n), struct(antennas + 8, n), jax.ShapeDtypeStruct(order.shape, order.dtype)),
        [HBM] * 4,
        [pltpu.VMEM(received.shape, F32), pltpu.SMEM((blocks,), F32), pltpu.SemaphoreType.DMA((5,))],
        8 << 20,
    )(outside(channel), outside(received), outside(noise_var), outside(order))
    tiles, group = n // TILE, len(planes[0])
    used = tiles * tiles // 2 * TILE + tiles * symbols + tiles // 2
    height = -(-used // group) * group
    take = lax.ppermute(give, "stripe", swap)
    own = call(functools.partial(gram, symbols), struct(height, TILE), [VMEM], flops=10**9)(keep)
    part = call(functools.partial(gram, symbols), struct(height, TILE), [VMEM, VMEM])(take, own)
    part = part.reshape(height, 1, TILE)
    part = lax.all_to_all(part, "stripe", 0, 0, axis_index_groups=planes, tiled=True)
    part = lax.optimization_barrier(part.reshape(height, TILE))
    part = jnp.sum(part.reshape(group, height // group, TILE), axis=0)
    part = lax.optimization_barrier(jnp.broadcast_to(part, (group, *part.shape)).reshape(height, TILE))
    part = part.reshape(height, 1, TILE)
    whole = lax.all_to_all(part, "stripe", 0, 0, axis_index_groups=planes, tiled=True)
    whole = whole.reshape(height, TILE)
    half = jax.ShapeDtypeStruct((n, n), BF16)
    diag, flag, x, e, v = call(
        functools.partial(invert, symbols),
        (struct(1, n), jax.ShapeDtypeStruct((1,), jnp.int32), half, half, half),
        [VMEM],
        [pltpu.VMEM((n, n), F32), pltpu.VMEM((2 * n, n), BF16)] + [pltpu.VMEM((n, n), F32)] * 3,
        outs_in=(VMEM, SMEM, VMEM, VMEM, VMEM),
    )(whole)
    rows = call(apply, struct(2 * symbols, n), [SMEM] + [VMEM] * 5, flops=10**9)(flag, whole, downlink, x, e, v)
    claimed, picked = call(
        functools.partial(claim, symbols),
        (struct(symbols + 8, n), struct(order.shape[1], symbols)),
        [VMEM] * 3,
        flops=10**8,
    )(rows, order, take)
    other = lax.ppermute(claimed, "stripe", swap)
    diag = diag + lax.ppermute(diag, "sub", cores)
    diag = diag + lax.ppermute(diag, ("stripe", "sub"), across)
    diag = diag + lax.ppermute(diag, "stripe", swap)
    transmit, owned = call(
        functools.partial(finish, blocks * subs),
        (struct(blocks, symbols, antennas), struct(blocks, order.shape[1], symbols)),
        [VMEM] * 5,
    )(rows, other, picked, diag, channel)
    return transmit, owned.transpose(0, 2, 1)


def solution(mesh):
    return jax.shard_map(
        shards,
        mesh=mesh,
        in_specs=(
            P("sub", "stripe", None, None),
            P("sub", None, "stripe"),
            P("sub", "stripe"),
            P("sub", None, None),
            P("stripe"),
        ),
        out_specs=(P("sub", None, "stripe"), P("sub", None, "stripe")),
        check_vma=False,
    )
```

```python
import functools

import jax
import jax.numpy as jnp
from jax import lax
from jax.experimental import pallas as pl
from jax.experimental.pallas import tpu as pltpu
from jax.sharding import PartitionSpec as P


prior_var = 0.1
TILE = 128
F32, BF16 = jnp.float32, jnp.bfloat16


def mm(left, right, dims=((1,), (0,))):
    return lax.dot_general(left, right, (dims, ((), ())), preferred_element_type=F32)


def exact(left, right):
    return jnp.dot(left, right, precision=lax.Precision.HIGHEST, preferred_element_type=F32)


def split(value):
    high = value.astype(BF16)
    return high, (value - high.astype(F32)).astype(BF16)


def kept_block():
    return lax.bitwise_and(lax.shift_right_logical(lax.axis_index("stripe"), 2), 1)


def enter(channel_ref, received_ref, noise_ref, order_ref, keep_ref, give_ref, kept_ref, samples, noise, sems):
    mine = kept_block()
    antennas = channel_ref.shape[1]
    sides = ((mine, keep_ref), (1 - mine, give_ref))
    copies = [
        pltpu.make_async_copy(received_ref, samples, sems.at[0]),
        pltpu.make_async_copy(noise_ref, noise, sems.at[1]),
        pltpu.make_async_copy(order_ref, kept_ref, sems.at[2]),
    ] + [
        pltpu.make_async_copy(channel_ref.at[which], out_ref.at[pl.ds(0, antennas)], sems.at[3 + k])
        for k, (which, out_ref) in enumerate(sides)
    ]
    for copy in copies:
        copy.start()
    for copy in copies[:2]:
        copy.wait()
    for which, out_ref in sides:
        out_ref[antennas:] = jnp.full((8, out_ref.shape[1]), noise[which], F32)
        for k in range(samples.shape[1] // 8):
            out_ref[antennas:, k * TILE : k * TILE + antennas] = samples[which, 8 * k : 8 * k + 8]
    copies[2].wait()
    give_ref[antennas : antennas + 1, order_lanes(antennas, order_ref.shape[1])] = kept_ref[...].astype(F32)
    for copy in copies[3:]:
        copy.wait()


def order_lanes(antennas, count):
    return slice(TILE + antennas, TILE + antennas + count)


def gram(symbols, block_ref, *rest):
    *base, out_ref = rest
    antennas, users = block_ref.shape[0] - 8, block_ref.shape[1]

    def put(at, value):
        rows = slice(at, at + value.shape[0])
        out_ref[rows] = base[0][rows] + value if base else value

    extra = block_ref[antennas:]
    scale = 1.0 / jnp.sqrt(extra[:1, antennas : antennas + 1])
    samples = jnp.concatenate([extra[:, k * TILE : k * TILE + antennas] for k in range(symbols // 8)], axis=0)
    high, low = split(block_ref[:antennas] * scale)
    left = jnp.concatenate([high, high, low], axis=0).T
    right = jnp.concatenate([high, low, high], axis=0)
    y_high, y_low = split(samples * scale)
    mixed = mm(jnp.concatenate([y_high, y_high, y_low], axis=1), right)
    tiles, at = users // TILE, 0
    lower = lower_of(TILE)
    diagonal = []
    for i in range(tiles):
        row = mm(left[i * TILE : (i + 1) * TILE], right[:, : (i + 1) * TILE])
        for j in range(i):
            put(at, row[:, j * TILE : (j + 1) * TILE])
            at += TILE
        diagonal.append(row[:, i * TILE :])
    for i in range(0, tiles, 2):
        put(at, jnp.where(lower, diagonal[i], diagonal[i + 1]))
        at += TILE
    for j in range(tiles):
        put(at, mixed[:, j * TILE : (j + 1) * TILE])
        at += symbols
    ends = [
        jnp.sum(jnp.where(eye_of(TILE), diagonal[i], 0.0), axis=0, keepdims=True) for i in range(1, tiles, 2)
    ]
    put(at, jnp.concatenate(ends + [jnp.zeros((out_ref.shape[0] - at - len(ends), TILE), F32)], axis=0))


def lower_of(n):
    return lax.broadcasted_iota(jnp.int32, (n, n), 0) >= lax.broadcasted_iota(jnp.int32, (n, n), 1)


def eye_of(n):
    return lax.broadcasted_iota(jnp.int32, (n, n), 0) == lax.broadcasted_iota(jnp.int32, (n, n), 1)


def after(bound):
    square = bound * bound
    return square / (2.0 - square)


def gain_of(bound):
    return 2.0 / (2.0 - bound * bound)


def invert(symbols, gram_ref, diag_ref, flag_ref, x_ref, e_ref, v_ref, a_ref, s_ref, t_ref, u_ref, w_ref):
    n = a_ref.shape[0]
    tiles, at = n // TILE, 0
    prior = 1.0 / prior_var
    lower, middle = lower_of(TILE), eye_of(TILE)
    tail = tiles * tiles // 2 * TILE + tiles * symbols

    def put(i, j, tile):
        a_ref[i * TILE : (i + 1) * TILE, j * TILE : (j + 1) * TILE] = tile

    for i in range(tiles):
        for j in range(i):
            tile = gram_ref[at : at + TILE]
            at += TILE
            put(i, j, tile)
            put(j, i, tile.T)
    for i in range(0, tiles, 2):
        tile = gram_ref[at : at + TILE]
        at += TILE
        flip = tile.T
        put(i, i, jnp.where(lower, tile, flip) + jnp.where(middle, prior, 0.0))
        row = gram_ref[tail + i // 2 : tail + i // 2 + 1] + prior
        put(i + 1, i + 1, jnp.where(middle, row, jnp.where(lower, flip, tile)))
    a = a_ref[...]
    eye = jnp.where(eye_of(n), 1.0, 0.0)
    top = jnp.max(jnp.sum(jnp.abs(a), axis=0, keepdims=True), axis=1, keepdims=True) * 1.0001
    alpha = 2.0 / (prior + top)
    start = (top - prior) / (top + prior)
    a_high, a_low = split(a)
    rounded = a_high.astype(F32)
    gain = alpha * gain_of(start)
    s_ref[n:] = ((2.0 * gain) * eye - (gain * alpha) * rounded).astype(BF16)

    def squared(product, bound):
        square = bound * bound
        scale = 1.0 / (2.0 - square)
        return ((2.0 * scale) * product - (square * scale) * eye).astype(BF16)

    scale = 2.0 * alpha / (2.0 - start * start)
    s_ref[:n] = (eye + (scale * alpha) * mm(a_high, a_high) - (2.0 * scale) * rounded).astype(BF16)
    first = after(start)
    bound, steps = first, jnp.zeros((1, 1), F32)
    for _ in range(10):
        bound = after(bound)
        steps = steps + jnp.where(bound > 0.0165, 1.0, 0.0)
    steps = jnp.max(steps).astype(jnp.int32)

    def step(index, bound):
        both = mm(s_ref[...], s_ref[:n])
        s_ref[n:] = (gain_of(bound) * (s_ref[n:].astype(F32) + both[n:])).astype(BF16)
        s_ref[:n] = squared(both[:n], bound)
        return after(bound)

    bound = lax.fori_loop(0, steps, step, first)
    x = s_ref[n:]
    x = (gain_of(bound) * (x.astype(F32) + mm(x, s_ref[:n]))).astype(BF16)
    x_ref[...] = x
    strips = [slice(at, at + 128) for at in range(0, n, 128)]
    parts = mm(jnp.concatenate([part for rows in strips for part in (a_high[rows], a_low[rows])], axis=0), x)
    for k, rows in enumerate(strips):
        product = parts[2 * k * 128 : (2 * k + 1) * 128] + parts[(2 * k + 1) * 128 : (2 * k + 2) * 128]
        e_ref[rows] = (eye[rows] - product).astype(BF16)
    e = e_ref[...]
    blocks = [slice(at, at + 128) for at in range(0, n, 128)]
    both = mm(jnp.concatenate([part for rows in blocks for part in (e[rows], x[rows])], axis=0), e)
    diag, size = jnp.zeros((1, n), F32), jnp.zeros((1, n), F32)
    for k, rows in enumerate(blocks):
        twice = both[2 * k * 128 : (2 * k + 1) * 128]
        update = both[(2 * k + 1) * 128 : (2 * k + 2) * 128]
        v_ref[rows] = twice.astype(BF16)
        own = jnp.where(eye[rows] > 0.0, x[rows].astype(F32) + update, 0.0)
        diag = diag + jnp.sum(own + (e[rows].astype(F32) + twice) * update, axis=0, keepdims=True)
        size = size + jnp.sum(twice * twice, axis=0, keepdims=True)
    diag_ref[...] = diag
    good = jnp.sum(size) < 6e-5
    flag_ref[0] = good.astype(jnp.int32)

    @pl.when(jnp.logical_not(good))
    def _():
        full(prior, top, start, a_ref, t_ref, u_ref, w_ref, diag_ref, x_ref, e_ref, v_ref)


def full(prior, top, start, a_ref, t_ref, u_ref, w_ref, diag_ref, x_ref, e_ref, v_ref):
    n = a_ref.shape[0]
    tiles = n // TILE

    def over(body):
        def one(index, carry):
            i, j = index // tiles, index % tiles
            rows, columns = (pl.ds(pl.multiple_of(k * TILE, TILE), TILE) for k in (i, j))
            body(rows, columns, jnp.where(eye_of(TILE) & (i == j), 1.0, 0.0))
            return carry

        lax.fori_loop(0, tiles * tiles, one, 0)

    gain = (2.0 / (prior + top)) * gain_of(start)

    def begin(rows, columns, eye):
        t_ref[rows, columns] = gain * (2.0 * eye - (2.0 / (prior + top)) * a_ref[rows, columns])

    over(begin)

    first = after(start)

    def more(index, carry):
        bound = after(carry[0])
        return bound, carry[1] + jnp.where(carry[0] > 1e-3, 1.0, 0.0)

    steps = lax.fori_loop(0, 40, more, (first, jnp.zeros((1, 1), F32)))[1]

    def step(index, bound):
        def residual(rows, columns, eye):
            u_ref[rows, columns] = eye - exact(a_ref[rows, :], t_ref[:, columns])

        def update(rows, columns, eye):
            w_ref[rows, columns] = gain_of(bound) * (t_ref[rows, columns] + exact(t_ref[rows, :], u_ref[:, columns]))

        def back(rows, columns, eye):
            t_ref[rows, columns] = w_ref[rows, columns]

        over(residual)
        over(update)
        over(back)
        return after(bound)

    lax.fori_loop(0, jnp.max(steps).astype(jnp.int32) + 2, step, first)
    diag_ref[...] = jnp.zeros(diag_ref.shape, F32)

    def finish(rows, columns, eye):
        x = t_ref[rows, columns]
        diag_ref[:, columns] = diag_ref[:, columns] + jnp.sum(x * eye, axis=0, keepdims=True)
        x_ref[rows, columns] = x.astype(BF16)
        e_ref[rows, columns], v_ref[rows, columns] = split(x - x.astype(BF16).astype(F32))

    over(finish)


def apply(flag_ref, gram_ref, downlink_ref, x_ref, e_ref, v_ref, rows_ref):
    symbols, n = downlink_ref.shape[1:]
    tiles = n // TILE
    at = tiles * tiles // 2 * TILE
    mixed = jnp.concatenate([gram_ref[at + symbols * j : at + symbols * (j + 1)] for j in range(tiles)], axis=1)
    rows = jnp.concatenate([downlink_ref[kept_block()], mixed], axis=0)
    good = flag_ref[0] == 1

    @pl.when(good)
    def _():
        high, low = split(rows)
        z = mm(jnp.concatenate([high, low], axis=0), x_ref[...])
        z = z[: 2 * symbols] + z[2 * symbols :]
        z = z + mm(z.astype(BF16), e_ref[...])
        rows_ref[...] = z + mm(z.astype(BF16), v_ref[...])

    @pl.when(jnp.logical_not(good))
    def _():
        x = x_ref[...].astype(F32) + (e_ref[...].astype(F32) + v_ref[...].astype(F32))
        rows_ref[...] = exact(rows, x)


def claim(symbols, rows_ref, order_ref, take_ref, give_ref, owned_ref):
    n, count = rows_ref.shape[1], order_ref.shape[1]
    antennas = take_ref.shape[0] - 8
    theirs = take_ref[antennas : antennas + 1, order_lanes(antennas, count)].astype(jnp.int32)
    order = jnp.concatenate([order_ref[...], theirs], axis=1)
    pick = (lax.broadcasted_iota(jnp.int32, (n, 2 * count), 0) == order).astype(BF16)
    x = rows_ref[symbols:]
    high = x.astype(BF16)
    middle, low = split(x - high.astype(F32))
    parts = mm(jnp.concatenate([high, middle, low], axis=0), pick)
    picked = (parts[:symbols] + (parts[symbols : 2 * symbols] + parts[2 * symbols :])).T
    owned_ref[...] = picked[:count]
    give_ref[:symbols] = rows_ref[:symbols]
    give_ref[symbols:] = jnp.zeros((8, n), F32)
    for k in range(count // 8):
        give_ref[symbols:, k * TILE : k * TILE + symbols] = picked[count + 8 * k : count + 8 * k + 8]


def finish(terms, own_ref, other_ref, mine_ref, diag_ref, channel_ref, transmit_ref, owned_ref):
    mine = kept_block()
    symbols, count = transmit_ref.shape[1], owned_ref.shape[1]
    mean_error = diag_ref[...] / terms
    scale = lax.rsqrt(mean_error)
    scale = scale * (1.5 - 0.5 * mean_error * scale * scale)
    for block, rows_ref in ((mine, own_ref), (1 - mine, other_ref)):
        high, low = split(rows_ref[:symbols] * scale)
        h_high, h_low = split(channel_ref[block])
        left = jnp.concatenate([high, low], axis=0)
        one = mm(left, h_high, ((1,), (1,)))
        two = mm(high, h_low, ((1,), (1,)))
        transmit_ref[block] = one[:symbols] + (one[symbols:] + two)
    owned_ref[mine] = mine_ref[...]
    theirs = [other_ref[symbols:, k * TILE : k * TILE + symbols] for k in range(count // 8)]
    owned_ref[1 - mine] = jnp.concatenate(theirs, axis=0)


VMEM = pl.BlockSpec(memory_space=pltpu.VMEM)
SMEM = pl.BlockSpec(memory_space=pltpu.SMEM)


HBM = pl.BlockSpec(memory_space=pltpu.HBM)


def call(body, outs, in_specs, scratch=(), grant=48 << 20, outs_in=None, flops=None):
    return pl.pallas_call(
        body,
        out_shape=outs,
        in_specs=in_specs,
        out_specs=outs_in or jax.tree.map(lambda _: VMEM, outs),
        cost_estimate=flops and pl.CostEstimate(flops=flops, bytes_accessed=2 << 20, transcendentals=0),
        scratch_shapes=scratch,
        compiler_params=pltpu.CompilerParams(vmem_limit_bytes=grant),
    )


def shards(channel, received, noise_var, downlink, user_order):
    blocks, _, antennas, n = channel.shape
    symbols = received.shape[1]
    channel = channel.reshape(blocks, antennas, n)
    noise_var = noise_var.reshape(blocks)
    order = user_order.reshape(1, -1)
    links, subs = lax.axis_size("stripe"), lax.axis_size("sub")
    pair, ring = 4, links // 8
    planes = [[x * 8 + y * pair + z for x in range(ring) for z in range(pair)] for y in range(2)]
    swap = [(i, i ^ pair) for i in range(links)]
    cores = [(i, i ^ 1) for i in range(subs)]
    across = [(i * subs + s, (i ^ pair) * subs + (s ^ 2)) for i in range(links) for s in range(subs)]

    def struct(*shape):
        return jax.ShapeDtypeStruct(shape, F32)

    def outside(value):
        return pltpu.with_memory_space_constraint(value, pltpu.HBM)

    keep, give, order = call(
        enter,
        (struct(antennas + 8, n), struct(antennas + 8, n), jax.ShapeDtypeStruct(order.shape, order.dtype)),
        [HBM] * 4,
        [pltpu.VMEM(received.shape, F32), pltpu.SMEM((blocks,), F32), pltpu.SemaphoreType.DMA((5,))],
        8 << 20,
    )(outside(channel), outside(received), outside(noise_var), outside(order))
    tiles, group = n // TILE, len(planes[0])
    used = tiles * tiles // 2 * TILE + tiles * symbols + tiles // 2
    height = -(-used // group) * group
    take = lax.ppermute(give, "stripe", swap)
    own = call(functools.partial(gram, symbols), struct(height, TILE), [VMEM], flops=10**9)(keep)
    part = call(functools.partial(gram, symbols), struct(height, TILE), [VMEM, VMEM])(take, own)
    part = part.reshape(height, 1, TILE)
    part = lax.all_to_all(part, "stripe", 0, 0, axis_index_groups=planes, tiled=True)
    part = lax.optimization_barrier(part.reshape(height, TILE))
    part = jnp.sum(part.reshape(group, height // group, TILE), axis=0)
    part = lax.optimization_barrier(jnp.broadcast_to(part, (group, *part.shape)).reshape(height, TILE))
    part = part.reshape(height, 1, TILE)
    whole = lax.all_to_all(part, "stripe", 0, 0, axis_index_groups=planes, tiled=True)
    whole = whole.reshape(height, TILE)
    half = jax.ShapeDtypeStruct((n, n), BF16)
    diag, flag, x, e, v = call(
        functools.partial(invert, symbols),
        (struct(1, n), jax.ShapeDtypeStruct((1,), jnp.int32), half, half, half),
        [VMEM],
        [pltpu.VMEM((n, n), F32), pltpu.VMEM((2 * n, n), BF16)] + [pltpu.VMEM((n, n), F32)] * 3,
        outs_in=(VMEM, SMEM, VMEM, VMEM, VMEM),
    )(whole)
    rows = call(apply, struct(2 * symbols, n), [SMEM] + [VMEM] * 5, flops=10**9)(flag, whole, downlink, x, e, v)
    claimed, picked = call(
        functools.partial(claim, symbols),
        (struct(symbols + 8, n), struct(order.shape[1], symbols)),
        [VMEM] * 3,
        flops=10**8,
    )(rows, order, take)
    other = lax.ppermute(claimed, "stripe", swap)
    diag = diag + lax.ppermute(diag, "sub", cores)
    diag = diag + lax.ppermute(diag, ("stripe", "sub"), across)
    diag = diag + lax.ppermute(diag, "stripe", swap)
    transmit, owned = call(
        functools.partial(finish, blocks * subs),
        (struct(blocks, symbols, antennas), struct(blocks, order.shape[1], symbols)),
        [VMEM] * 5,
    )(rows, other, picked, diag, channel)
    return transmit, owned.transpose(0, 2, 1)


def solution(mesh):
    return jax.shard_map(
        shards,
        mesh=mesh,
        in_specs=(
            P("sub", "stripe", None, None),
            P("sub", None, "stripe"),
            P("sub", "stripe"),
            P("sub", None, None),
            P("stripe"),
        ),
        out_specs=(P("sub", None, "stripe"), P("sub", None, "stripe")),
        check_vma=False,
    )
```
